32 devices in a mesh: pipe: 4 (over y, core), expert: 8 (over z, x).
Axes of the slice: x: 2, y: 2, z: 4, core: 2. Of those that a mesh axis runs over, the one named last changes fastest.
Arguments:
- layer_input: bfloat16 [4, 512, 2880], P('pipe', 'expert'), may hold values from -6 to 6
- grad_output: bfloat16 [4, 512, 2880], P('pipe', 'expert'), may hold values from -6 to 6
- expert_ids: int32 [4, 512, 4], P('pipe', 'expert'), may hold values from 0 to 127, as said below
- gate_probs: float32 [4, 512, 4], P('pipe', 'expert'), may hold values from 0.05 to 1
- w_gate: bfloat16 [4, 2880, 2880], P('pipe', 'expert'), may hold values from -0.109375 to 0.109375
- w_up: bfloat16 [4, 2880, 2880], P('pipe', 'expert'), may hold values from -0.109375 to 0.109375
- w_down: bfloat16 [4, 2880, 2880], P('pipe', 'expert'), may hold values from -0.109375 to 0.109375
Outputs:
- grad_gate: bfloat16 [4, 2880, 2880], P('pipe', 'expert')
- grad_up: bfloat16 [4, 2880, 2880], P('pipe', 'expert')
- grad_down: bfloat16 [4, 2880, 2880], P('pipe', 'expert')
- grad_prev: bfloat16 [4, 512, 2880], P('pipe', 'expert')
The draws below stay inside these ranges and needn't reach their ends.
Inputs may be any that keep to these rules, and one draw needn't show every extreme that they name: `expert_ids`: in each section, within the 64 tokens of one device, no expert is named by more than 4 tokens; in each section one expert below 1, the same for all devices of that section, is named by exactly 4 tokens of every device; a token names 4 different experts.
All inputs are finite; a program needn't handle non-finite values.
Results may differ from the reference program's by a relative error of at most 0.0085.
Values may be sent and summed in bfloat16 or wider, within the bound.
No kernel may reach another device: no remote copies, remote signals or barrier semaphores. Data moves between devices by JAX's collectives and lax.ppermute only.
A program may use at most 64 MiB of HBM per device.

```python
import math
from functools import partial
import jax
import jax.numpy as jnp
from jax import lax

D = 2880
FF = 2880
EXPERTS = 128
TOPK = 4
SLICES = 8
TOK_DEV = 64
CAP = 4
HS = 360
FLIGHT = 1
TOKENS = 512
N_PIPE = 4


def route_block(block_key, shifts):
    jitter_key, order_key, token_key = jax.random.split(block_key, 3)
    tickets = EXPERTS * CAP
    jitter = jax.random.randint(jitter_key, (EXPERTS, CAP), 0, 65536).astype(jnp.int32)
    scores = (shifts[:, None] + jitter) * tickets + jnp.arange(tickets, dtype=jnp.int32).reshape(EXPERTS, CAP)
    values_top, picked = lax.top_k(scores.reshape(tickets), TOK_DEV * TOPK)
    picked = picked.astype(jnp.int32)
    owners = picked // CAP
    within = picked % CAP
    shuffled = jax.random.permutation(order_key, EXPERTS).astype(jnp.int32)
    position = jnp.argsort(shuffled, stable=True).astype(jnp.int32)
    arranged = owners[jnp.argsort(position[owners] * CAP + within, stable=True)]
    layout = arranged.reshape(TOPK, TOK_DEV).T
    return layout[jax.random.permutation(token_key, TOK_DEV)]


def route_section(section_key):
    level_key, favored_key, rest_key = jax.random.split(section_key, 3)
    blocks = TOKENS // TOK_DEV
    levels = jax.random.randint(level_key, (EXPERTS,), 0, 4).astype(jnp.int32)
    favored = jax.random.randint(favored_key, (), 0, FLIGHT).astype(jnp.int32)
    shifts = jnp.where(jnp.arange(EXPERTS, dtype=jnp.int32) == favored, 262144, levels * 16384).astype(jnp.int32)
    block_keys = jax.random.split(rest_key, blocks)
    routed = jax.vmap(partial(route_block, shifts=shifts))(block_keys)
    return routed.reshape(blocks * TOK_DEV, TOPK)


def draw_expert_ids(key, part):
    folded = jax.random.fold_in(key, 7)
    section_keys = jax.random.split(folded, N_PIPE)
    return jax.vmap(route_section)(section_keys).astype(jnp.int32)


def block_scale(rng, dims, cuts, low, high):
    def one(dim, parts):
        steps = jax.random.uniform(jax.random.fold_in(jax.random.fold_in(rng, 6), dim), (parts,), jnp.float32, low / len(cuts), high / len(cuts))
        return jnp.repeat(jnp.exp(steps), dims[dim] // parts).reshape((-1,) + (1,) * (len(dims) - dim - 1))

    loudness = one(*cuts[0])
    for cut in cuts[1:]:
        loudness = loudness * one(*cut)
    return loudness


def bell_draw(stream_key, shape, scale, limit, pieces=(), kind=jnp.bfloat16):
    result = scale * jax.random.normal(stream_key, shape, jnp.float32)
    if pieces:
        result = result * block_scale(stream_key, shape, pieces, -0.22, 0.18)
    return jnp.clip(result, -limit, limit).astype(kind)


def setup_inputs(seed: int = 0) -> dict:
    keys = jax.random.split(jax.random.key(seed), 8)
    layer_input = bell_draw(keys[0], (N_PIPE, TOKENS, D), 1.0, 6.0, ((0, 4), (1, 8)))
    grad_output = bell_draw(keys[1], (N_PIPE, TOKENS, D), 1.0, 6.0, ((0, 4), (1, 8)))
    expert_ids = draw_expert_ids(jax.random.fold_in(keys[7], 71), 0)
    gate_probs = jnp.clip(jnp.exp(math.log(1.0) - 2.9957323 * jax.random.uniform(keys[3], (N_PIPE, TOKENS, TOPK), jnp.float32) ** block_scale(keys[3], (N_PIPE, TOKENS, TOPK), ((0, 4), (1, 8)), -0.2, 0.2)), 0.05, 1.0)
    w_gate = bell_draw(keys[4], (N_PIPE, FLIGHT * FF, D), D ** -0.5, 0.109375, ((0, 4), (1, 8)))
    w_up = bell_draw(keys[5], (N_PIPE, FLIGHT * FF, D), D ** -0.5, 0.109375, ((0, 4), (1, 8)))
    w_down = bell_draw(keys[6], (N_PIPE, FLIGHT * FF, D), FF ** -0.5, 0.109375, ((0, 4), (1, 8)))
    return {"layer_input": layer_input, "grad_output": grad_output, "expert_ids": expert_ids, "gate_probs": gate_probs, "w_gate": w_gate, "w_up": w_up, "w_down": w_down}


def silu_parts(pre_gate):
    sigma = jax.nn.sigmoid(pre_gate)
    return pre_gate * sigma, sigma * (1.0 + pre_gate * (1.0 - sigma))


def contract_first(left, right):
    return lax.dot_general(left, right, (((0,), (0,)), ((), ())), preferred_element_type=jnp.float32)


def contract_last(left, right):
    return lax.dot_general(left, right, (((1,), (1,)), ((), ())), preferred_element_type=jnp.float32)


def reference(layer_input, grad_output, expert_ids, gate_probs, w_gate, w_up, w_down):
    sections = layer_input.shape[0]
    total = layer_input.shape[1]
    flight = w_gate.shape[1] // FF
    blocks = total // TOK_DEV
    buffer_rows = blocks * CAP
    gate_all, up_all, down_all, input_all = [], [], [], []
    for section in range(sections):
        inputs = layer_input[section]
        cotan = grad_output[section]
        scaled = (gate_probs[section][:, :, None] * cotan[:, None, :].astype(jnp.float32)).astype(jnp.bfloat16)
        input_grad = jnp.zeros((total, D), jnp.float32)
        gate_list, up_list, down_list = [], [], []
        for expert in range(flight):
            matched = expert_ids[section] == expert
            hit = jnp.any(matched, axis=1)
            picked = jnp.sum(jnp.where(matched[:, :, None], scaled.astype(jnp.float32), 0.0), axis=1).astype(jnp.bfloat16)
            hit_int = hit.astype(jnp.int32).reshape(blocks, TOK_DEV)
            ranks = jnp.cumsum(hit_int, axis=1) - 1
            base = (jnp.arange(blocks, dtype=jnp.int32) * CAP)[:, None]
            target = jnp.where(hit_int > 0, base + ranks, buffer_rows).reshape(total).astype(jnp.int32)
            in_rows = jnp.zeros((buffer_rows, D), jnp.bfloat16).at[target].set(inputs, mode="drop")
            co_rows = jnp.zeros((buffer_rows, D), jnp.bfloat16).at[target].set(picked, mode="drop")
            weight_gate = w_gate[section, expert * FF:(expert + 1) * FF]
            weight_up = w_up[section, expert * FF:(expert + 1) * FF]
            weight_down = w_down[section, expert * FF:(expert + 1) * FF]
            pre_gate = contract_last(in_rows, weight_gate)
            pre_up = contract_last(in_rows, weight_up)
            silu_val, silu_grad = silu_parts(pre_gate)
            hidden = (silu_val * pre_up).astype(jnp.bfloat16)
            hidden_grad = contract_last(co_rows, weight_down)
            grad_pre_gate = (hidden_grad * pre_up * silu_grad).astype(jnp.bfloat16)
            grad_pre_up = (hidden_grad * silu_val).astype(jnp.bfloat16)
            down_list.append(contract_first(hidden, co_rows).astype(jnp.bfloat16))
            gate_list.append(contract_first(grad_pre_gate, in_rows).astype(jnp.bfloat16))
            up_list.append(contract_first(grad_pre_up, in_rows).astype(jnp.bfloat16))
            partial_value = jnp.einsum("rsh,shd->rsd", grad_pre_gate.astype(jnp.float32).reshape(buffer_rows, SLICES, HS),
                                 weight_gate.astype(jnp.float32).reshape(SLICES, HS, D), precision=lax.Precision.HIGHEST)
            partial_value = partial_value + jnp.einsum("rsh,shd->rsd", grad_pre_up.astype(jnp.float32).reshape(buffer_rows, SLICES, HS),
                                           weight_up.astype(jnp.float32).reshape(SLICES, HS, D), precision=lax.Precision.HIGHEST)
            combined = jnp.sum(partial_value.astype(jnp.bfloat16).astype(jnp.float32), axis=1)
            safe_target = jnp.minimum(target, buffer_rows - 1)
            input_grad = input_grad + jnp.where(hit[:, None], combined[safe_target], 0.0)
        gate_all.append(jnp.concatenate(gate_list, axis=0))
        up_all.append(jnp.concatenate(up_list, axis=0))
        down_all.append(jnp.concatenate(down_list, axis=0))
        input_all.append(input_grad.astype(jnp.bfloat16))
    shifted = input_all[1:] + [jnp.zeros((total, D), jnp.bfloat16)]
    return jnp.stack(gate_all), jnp.stack(up_all), jnp.stack(down_all), jnp.stack(shifted)
```

```python
import functools

import jax
import jax.numpy as jnp
from jax import lax
from jax.experimental import pallas as pl
from jax.experimental.pallas import tpu as pltpu
from jax.sharding import PartitionSpec as P

SLICES = 8
CAP = 4
PAIR = 2 * CAP
LANES = 128

VMEM = pl.BlockSpec(memory_space=pltpu.VMEM)


def contract_last(left, right):
    return lax.dot_general(
        left, right, (((1,), (1,)), ((), ())), preferred_element_type=jnp.float32
    )


def contract_first(left, right):
    return lax.dot_general(
        left, right, (((0,), (0,)), ((), ())), preferred_element_type=jnp.float32
    )


def select_kernel(flight, ids_ref, probs_ref, input_ref, cotan_ref, rows_ref, slots_ref):
    ids = ids_ref[...]
    probs = probs_ref[...]
    tokens = ids.shape[1]
    before = lax.broadcasted_iota(jnp.int32, (tokens, tokens), 0) < lax.broadcasted_iota(
        jnp.int32, (tokens, tokens), 1
    )
    before = before.astype(jnp.float32).astype(jnp.bfloat16)
    row = lax.broadcasted_iota(jnp.int32, (PAIR, tokens), 0)
    token = lax.broadcasted_iota(jnp.int32, (PAIR, tokens), 1).astype(jnp.float32)
    slot = lax.rem(row, CAP)
    for expert in range(flight):
        matched = ids == expert
        hit = jnp.sum(jnp.where(matched, 1.0, 0.0), axis=0, keepdims=True)
        prob = jnp.sum(jnp.where(matched, probs, 0.0), axis=0, keepdims=True)
        hits = jnp.broadcast_to(hit, (PAIR, tokens))
        ranks = jnp.dot(hits.astype(jnp.bfloat16), before, preferred_element_type=jnp.float32)
        chosen = jnp.where((hits > 0.5) & (ranks.astype(jnp.int32) == slot), 1.0, 0.0)
        scale = jnp.sum(chosen * prob, axis=1, keepdims=True)
        number = jnp.sum(chosen * token, axis=1, keepdims=True)
        chooser = chosen.astype(jnp.bfloat16)
        taken = jnp.dot(chooser, input_ref[...], preferred_element_type=jnp.float32)
        cotan = jnp.dot(chooser, cotan_ref[...], preferred_element_type=jnp.float32) * scale
        wide = lax.broadcasted_iota(jnp.int32, taken.shape, 0) < CAP
        rows_ref[pl.ds(expert * PAIR, PAIR), :] = jnp.where(wide, taken, cotan).astype(
            jnp.bfloat16
        )
        slots_ref[pl.ds(expert * PAIR, PAIR), :] = jnp.broadcast_to(number, (PAIR, LANES))


def select_rows(ids, probs, inputs, cotan, flight):
    width = inputs.shape[1]
    return pl.pallas_call(
        functools.partial(select_kernel, flight),
        out_shape=(
            jax.ShapeDtypeStruct((flight * PAIR, width), jnp.bfloat16),
            jax.ShapeDtypeStruct((flight * PAIR, LANES), jnp.float32),
        ),
        in_specs=[VMEM] * 4,
        out_specs=(VMEM, VMEM),
        compiler_params=pltpu.CompilerParams(vmem_limit_bytes=8 << 20),
        name="select",
    )(ids, probs, inputs, cotan)


def main_kernel(pieces, split, *refs):
    row_refs, (gate_ref, up_ref, down_ref) = refs[:pieces], refs[pieces : pieces + 3]
    all_ref, gate_out, up_out, hidden_out = refs[pieces + 3 : pieces + 7]
    partial_refs = refs[pieces + 7 :]
    start = 0
    for ref in row_refs:
        all_ref[pl.ds(start, ref.shape[0]), :] = ref[...]
        start += ref.shape[0]
    rows = all_ref[...]
    total = rows.shape[0]
    pre_gate = contract_last(rows, gate_ref[...])
    pre_up = contract_last(rows, up_ref[...])
    hidden_grad = pltpu.roll(contract_last(rows, down_ref[...]), total - CAP, 0)
    sigma = jax.nn.sigmoid(pre_gate)
    silu_val = pre_gate * sigma
    silu_grad = sigma * (1.0 + pre_gate * (1.0 - sigma))
    first = lax.rem(lax.broadcasted_iota(jnp.int32, pre_gate.shape, 0), PAIR) < CAP
    hidden = jnp.where(first, silu_val * pre_up, 0.0)
    grad_gate = jnp.where(first, hidden_grad * pre_up * silu_grad, 0.0)
    grad_up = jnp.where(first, hidden_grad * silu_val, 0.0)
    gate_out[...] = grad_gate.astype(jnp.bfloat16)
    up_out[...] = grad_up.astype(jnp.bfloat16)
    hidden_out[...] = pltpu.roll(hidden, CAP, 0).astype(jnp.bfloat16)

    def packed(value):
        blocks = total // PAIR
        moved = pltpu.roll(value, CAP, 0)
        return jnp.concatenate(
            [
                value[2 * m * PAIR : (2 * m + 1) * PAIR]
                + moved[(2 * m + 1) * PAIR : (2 * m + 2) * PAIR]
                for m in range(blocks // 2)
            ],
            axis=0,
        ).astype(jnp.bfloat16)

    partial = jnp.dot(packed(grad_gate), gate_ref[...], preferred_element_type=jnp.float32)
    partial = partial + jnp.dot(
        packed(grad_up), up_ref[...], preferred_element_type=jnp.float32
    )
    if split:
        half = partial.shape[0] // 2
        partial_refs[0][...] = partial[:half]
        partial_refs[1][...] = partial[half:].astype(jnp.bfloat16)
    else:
        partial_refs[0][...] = partial.astype(jnp.bfloat16)


def expert_main(pieces, weight_gate, weight_up, weight_down, split):
    total = sum(piece.shape[0] for piece in pieces)
    units, width = weight_gate.shape
    rows = total // 2
    small = jax.ShapeDtypeStruct((total, units), jnp.bfloat16)
    if split:
        partials = (
            jax.ShapeDtypeStruct((rows // 2, width), jnp.float32),
            jax.ShapeDtypeStruct((rows // 2, width), jnp.bfloat16),
        )
    else:
        partials = (jax.ShapeDtypeStruct((rows, width), jnp.bfloat16),)
    outs = (jax.ShapeDtypeStruct((total, width), jnp.bfloat16), small, small, small) + partials
    return pl.pallas_call(
        functools.partial(main_kernel, len(pieces), split),
        out_shape=outs,
        in_specs=[VMEM] * (len(pieces) + 3),
        out_specs=(VMEM,) * len(outs),
        compiler_params=pltpu.CompilerParams(vmem_limit_bytes=32 << 20),
        cost_estimate=pl.CostEstimate(
            flops=2 * total * units * width * 5,
            bytes_accessed=3 * units * width * 2,
            transcendentals=total * units,
        ),
        name="expert_main",
    )(*pieces, weight_gate, weight_up, weight_down)


def grad_kernel(left_ref, rows_ref, out_ref, turned_ref):
    step = pl.program_id(0)
    size = out_ref.shape[0]

    @pl.when(step == 0)
    def _():
        turned_ref[...] = left_ref[...].astype(jnp.float32).T.astype(jnp.bfloat16)

    left = turned_ref[pl.ds(pl.multiple_of(step * size, 8), size), :]
    out_ref[...] = jnp.dot(left, rows_ref[...], preferred_element_type=jnp.float32).astype(
        jnp.bfloat16
    )


def weight_grad(left, rows):
    total, units = left.shape
    width = rows.shape[1]
    steps = 3 if units % 24 == 0 else 1
    return pl.pallas_call(
        grad_kernel,
        out_shape=jax.ShapeDtypeStruct((units, width), jnp.bfloat16),
        grid=(steps,),
        in_specs=[
            pl.BlockSpec((total, units), lambda i: (0, 0)),
            pl.BlockSpec((total, width), lambda i: (0, 0)),
        ],
        out_specs=pl.BlockSpec((units // steps, width), lambda i: (i, 0)),
        scratch_shapes=[pltpu.VMEM((units, total), jnp.bfloat16)],
        compiler_params=pltpu.CompilerParams(vmem_limit_bytes=16 << 20),
        cost_estimate=pl.CostEstimate(
            flops=2 * total * units * width, bytes_accessed=units * width * 2, transcendentals=0
        ),
        name="weight_grad",
    )(left, rows)


def expand_kernel(message_ref, out_ref):
    message = message_ref[...]
    width = out_ref.shape[1]
    tokens = out_ref.shape[0]
    numbers = message[:, width : width + 1].astype(jnp.float32)
    column = lax.broadcasted_iota(jnp.int32, (CAP, tokens), 1).astype(jnp.float32)
    chooser = jnp.where(column == numbers, 1.0, 0.0).astype(jnp.bfloat16)
    out_ref[...] = contract_first(chooser, message[:, :width]).astype(jnp.bfloat16)


def expand(message, tokens, width):
    return pl.pallas_call(
        expand_kernel,
        out_shape=jax.ShapeDtypeStruct((tokens, width), jnp.bfloat16),
        in_specs=[VMEM],
        out_specs=VMEM,
        compiler_params=pltpu.CompilerParams(vmem_limit_bytes=8 << 20),
        name="expand",
    )(message)


def swap(value, bits):
    peers = lax.axis_size("expert")
    return lax.ppermute(value, "expert", [(i, i ^ bits) for i in range(peers)])


def shift_back(value):
    count = lax.axis_size("pipe")
    return lax.ppermute(value, "pipe", [(source, source - 1) for source in range(1, count)])


def body(layer_input, grad_output, expert_ids, gate_probs, w_gate, w_up, w_down):
    peers = lax.axis_size("expert")
    flight = peers // SLICES
    tokens, width = layer_input.shape[1:]
    ids = expert_ids[0].T
    probs = gate_probs[0].T
    own, slots = select_rows(ids, probs, layer_input[0], grad_output[0], flight)
    weights = (w_gate[0], w_up[0], w_down[0])
    if flight == 1:
        far, near, end = swap(own, 4), swap(own, 2), swap(own, 6)
        across = swap(jnp.concatenate([own, far, near], axis=0), 1)
        across_end = swap(end, 1)
        pieces = (own, far, near, end, across, across_end)
        rows, gate, up, hidden, keep, send = expert_main(pieces, *weights, split=True)
        beside = swap(send, 1)
        grad_gate = weight_grad(gate, rows)
        grad_up = weight_grad(up, rows)
        grad_down = weight_grad(hidden, rows)
        summed = keep + beside.astype(jnp.float32)
        rounded = summed.astype(jnp.bfloat16)
        home = [
            swap(rounded[j * CAP : (j + 1) * CAP], bits).astype(jnp.float32)
            for j, bits in ((1, 4), (2, 2), (3, 6))
        ]
        combined = summed[:CAP] + home[0] + home[1] + home[2]
        message = jnp.concatenate([combined, slots[:CAP]], axis=1).astype(jnp.bfloat16)
        shifted = expand(shift_back(message), tokens, width)
    else:
        own = own.reshape(flight, PAIR, width)
        spread = jnp.repeat(own, SLICES, axis=0)
        received = lax.all_to_all(spread, "expert", split_axis=0, concat_axis=0, tiled=True)
        received = received.reshape(peers * PAIR, width)
        rows, gate, up, hidden, partial = expert_main((received,), *weights, split=False)
        partial = partial.reshape(peers, CAP, width)
        returned = lax.all_to_all(partial, "expert", split_axis=0, concat_axis=0, tiled=True)
        grad_gate = weight_grad(gate, rows)
        grad_up = weight_grad(up, rows)
        grad_down = weight_grad(hidden, rows)
        combined = jnp.sum(
            returned.astype(jnp.float32).reshape(flight, SLICES, CAP, width), axis=1
        ).reshape(flight * CAP, width)
        labels = jnp.arange(flight, dtype=jnp.int32)
        named = jnp.any(ids[None] == labels[:, None, None], axis=1)
        ranks = jnp.cumsum(named.astype(jnp.int32), axis=1) - 1
        slot = jnp.arange(CAP, dtype=jnp.int32)
        chooser = named[:, None, :] & (ranks[:, None, :] == slot[None, :, None])
        chooser = chooser.reshape(flight * CAP, tokens).astype(jnp.float32)
        input_grad = lax.dot_general(
            chooser,
            combined,
            (((0,), (0,)), ((), ())),
            precision=lax.Precision.HIGHEST,
            preferred_element_type=jnp.float32,
        )
        shifted = shift_back(input_grad.astype(jnp.bfloat16))
    return grad_gate[None], grad_up[None], grad_down[None], shifted[None]


def solution(mesh):
    spec = P("pipe", "expert", None)
    return jax.shard_map(
        body, mesh=mesh, in_specs=(spec,) * 7, out_specs=(spec,) * 4, check_vma=False
    )
```

```python
import functools

import jax
import jax.numpy as jnp
from jax import lax
from jax.experimental import pallas as pl
from jax.experimental.pallas import tpu as pltpu
from jax.sharding import PartitionSpec as P


SLICES = 8
CAP = 4
PAIR = 2 * CAP
LANES = 128
CHUNK = 1024
OUT = (6, 4, 2)
HOME = (4, 6, 2)

VMEM = pl.BlockSpec(memory_space=pltpu.VMEM)
HBM = pl.BlockSpec(memory_space=pl.ANY)


def contract_last(left, right):
    return lax.dot_general(
        left, right, (((1,), (1,)), ((), ())), preferred_element_type=jnp.float32
    )


def contract_first(left, right):
    return lax.dot_general(
        left, right, (((0,), (0,)), ((), ())), preferred_element_type=jnp.float32
    )


def select_kernel(flight, *refs):
    routes_ref, sources = refs[0], refs[1:3]
    (rows_ref, slots_ref), held, sems = refs[3:5], refs[5:7], refs[7]
    copies = [
        pltpu.make_async_copy(source, target, sems.at[i])
        for i, (source, target) in enumerate(zip(sources, held))
    ]
    for copy in copies:
        copy.start()
    ids = routes_ref[0]
    probs = routes_ref[1]
    tokens = ids.shape[1]
    before = lax.broadcasted_iota(jnp.int32, (tokens, tokens), 0) < lax.broadcasted_iota(
        jnp.int32, (tokens, tokens), 1
    )
    before = before.astype(jnp.float32).astype(jnp.bfloat16)
    row = lax.broadcasted_iota(jnp.int32, (PAIR, tokens), 0)
    token = lax.broadcasted_iota(jnp.int32, (PAIR, tokens), 1).astype(jnp.float32)
    slot = lax.rem(row, CAP)
    choosers = []
    for expert in range(flight):
        matched = ids == float(expert)
        hit = jnp.sum(jnp.where(matched, 1.0, 0.0), axis=0, keepdims=True)
        prob = jnp.sum(jnp.where(matched, probs, 0.0), axis=0, keepdims=True)
        hits = jnp.broadcast_to(hit, (PAIR, tokens))
        ranks = jnp.dot(hits.astype(jnp.bfloat16), before, preferred_element_type=jnp.float32)
        chosen = jnp.where((hits > 0.5) & (ranks.astype(jnp.int32) == slot), 1.0, 0.0)
        scale = jnp.sum(chosen * prob, axis=1, keepdims=True)
        number = jnp.sum(chosen * token, axis=1, keepdims=True)
        slots_ref[pl.ds(expert * PAIR, PAIR), :] = jnp.broadcast_to(number, (PAIR, LANES))
        choosers.append((chosen.astype(jnp.bfloat16), scale))
    for copy in copies:
        copy.wait()
    for expert, (chooser, scale) in enumerate(choosers):
        taken = jnp.dot(chooser, held[0][...], preferred_element_type=jnp.float32)
        cotan = jnp.dot(chooser, held[1][...], preferred_element_type=jnp.float32) * scale
        wide = lax.broadcasted_iota(jnp.int32, taken.shape, 0) < CAP
        rows_ref[pl.ds(expert * PAIR, PAIR), :] = jnp.where(wide, taken, cotan).astype(
            jnp.bfloat16
        )


def select_rows(ids, probs, inputs, cotan, flight):
    width = inputs.shape[1]
    plane = lax.broadcasted_iota(jnp.int32, (2, *ids.shape), 0)
    routes = jnp.where(plane == 0, ids.astype(jnp.float32)[None], probs[None])
    return pl.pallas_call(
        functools.partial(select_kernel, flight),
        out_shape=(
            jax.ShapeDtypeStruct((flight * PAIR, width), jnp.bfloat16),
            jax.ShapeDtypeStruct((flight * PAIR, LANES), jnp.float32),
        ),
        in_specs=[VMEM, HBM, HBM],
        out_specs=(VMEM, VMEM),
        scratch_shapes=[pltpu.VMEM(value.shape, value.dtype) for value in (inputs, cotan)]
        + [pltpu.SemaphoreType.DMA((2,))],
        compiler_params=pltpu.CompilerParams(vmem_limit_bytes=55000 << 10),
        name="select",
    )(routes, inputs, cotan)


def fetch_kernel(after_ref, *refs):
    del after_ref
    count = len(refs) // 2
    copies = [
        pltpu.make_async_copy(refs[i], refs[count + i], refs[-1].at[i]) for i in range(count)
    ]
    for copy in copies:
        copy.start()
    for copy in copies:
        copy.wait()


def fetch(after, *weights):
    held = sum(w.size * w.dtype.itemsize for w in weights)
    return pl.pallas_call(
        fetch_kernel,
        out_shape=tuple(jax.ShapeDtypeStruct(w.shape, w.dtype) for w in weights),
        in_specs=[HBM] * (len(weights) + 1),
        out_specs=(VMEM,) * len(weights),
        scratch_shapes=[pltpu.SemaphoreType.DMA((len(weights),))],
        compiler_params=pltpu.CompilerParams(vmem_limit_bytes=47600 << 10),
        cost_estimate=pl.CostEstimate(
            flops=0,
            bytes_accessed=sum(2 * w.size * w.dtype.itemsize for w in weights),
            transcendentals=0,
        ),
        name="fetch",
    )(after, *weights)


def main_kernel(pieces, split, *refs):
    row_refs, refs = refs[:pieces], refs[pieces:]
    slots_ref, gate_ref, up_ref, down_ref = refs[:4]
    all_ref, gate_out, up_out, hidden_out = refs[4:8]
    partial_refs = refs[8:]
    start = 0
    for ref in row_refs:
        all_ref[pl.ds(start, ref.shape[0]), :] = ref[...]
        start += ref.shape[0]
    rows = all_ref[...]
    total = rows.shape[0]
    pre_gate = contract_last(rows, gate_ref[...])
    pre_up = contract_last(rows, up_ref[...])
    hidden_grad = pltpu.roll(contract_last(rows, down_ref[...]), total - CAP, 0)
    sigma = jax.nn.sigmoid(pre_gate)
    silu_val = pre_gate * sigma
    silu_grad = sigma * (1.0 + pre_gate * (1.0 - sigma))
    first = lax.rem(lax.broadcasted_iota(jnp.int32, pre_gate.shape, 0), PAIR) < CAP
    hidden = jnp.where(first, silu_val * pre_up, 0.0)
    grad_gate = jnp.where(first, hidden_grad * pre_up * silu_grad, 0.0)
    grad_up = jnp.where(first, hidden_grad * silu_val, 0.0)
    gate_out[...] = grad_gate.astype(jnp.bfloat16)
    up_out[...] = grad_up.astype(jnp.bfloat16)
    hidden_out[...] = pltpu.roll(hidden, CAP, 0).astype(jnp.bfloat16)

    def packed(value):
        blocks = total // PAIR
        moved = pltpu.roll(value, CAP, 0)
        return jnp.concatenate(
            [
                value[2 * m * PAIR : (2 * m + 1) * PAIR]
                + moved[(2 * m + 1) * PAIR : (2 * m + 2) * PAIR]
                for m in range(blocks // 2)
            ],
            axis=0,
        ).astype(jnp.bfloat16)

    partial = jnp.dot(packed(grad_gate), gate_ref[...], preferred_element_type=jnp.float32)
    partial = partial + jnp.dot(
        packed(grad_up), up_ref[...], preferred_element_type=jnp.float32
    )
    if split:
        half, width = partial.shape[0] // 2, partial.shape[1]
        keep_ref, send_ref = partial_refs
        send_ref[...] = partial[half:].astype(jnp.bfloat16)
        keep_ref[:, :width] = partial[:half].astype(jnp.bfloat16)
        keep_ref[:PAIR, width:] = slots_ref[...].astype(jnp.bfloat16)
        keep_ref[PAIR:, width:] = jnp.zeros((half - PAIR, LANES), jnp.bfloat16)
    else:
        partial_refs[0][...] = partial.astype(jnp.bfloat16)


def expert_main(pieces, slots, weight_gate, weight_up, weight_down, split):
    total = sum(piece.shape[0] for piece in pieces)
    units, width = weight_gate.shape
    rows = total // 2
    small = jax.ShapeDtypeStruct((total, units), jnp.bfloat16)
    if split:
        partials = (
            jax.ShapeDtypeStruct((rows // 2, width + LANES), jnp.bfloat16),
            jax.ShapeDtypeStruct((rows // 2, width), jnp.bfloat16),
        )
    else:
        partials = (jax.ShapeDtypeStruct((rows, width), jnp.bfloat16),)
    outs = (jax.ShapeDtypeStruct((total, width), jnp.bfloat16), small, small, small) + partials
    return pl.pallas_call(
        functools.partial(main_kernel, len(pieces), split),
        out_shape=outs,
        in_specs=[VMEM] * (len(pieces) + 4),
        out_specs=(VMEM,) * len(outs),
        compiler_params=pltpu.CompilerParams(vmem_limit_bytes=32 << 20),
        cost_estimate=pl.CostEstimate(
            flops=2 * total * units * width * 5,
            bytes_accessed=3 * units * width * 2,
            transcendentals=total * units,
        ),
        name="expert_main",
    )(*pieces, slots, weight_gate, weight_up, weight_down)


def grad_kernel(count, *refs):
    lefts, rows_ref, outs = refs[:count], refs[count], refs[count + 1 : 2 * count + 1]
    held_ref, sems = refs[2 * count + 1 :]
    width = rows_ref.shape[1]
    copies = []
    for j in range(count):
        left = lefts[j][...]
        for c, start in enumerate(range(0, width, CHUNK)):
            part = pl.ds(start, min(CHUNK, width - start))
            held_ref[j, :, part] = contract_first(left, rows_ref[:, part]).astype(jnp.bfloat16)
            copy = pltpu.make_async_copy(
                held_ref.at[j, :, part], outs[j].at[:, part], sems.at[j, c]
            )
            copy.start()
            copies.append(copy)
    for copy in copies:
        copy.wait()


def weight_grads(rows, *lefts):
    total, width = rows.shape
    units = lefts[0].shape[1]
    count = len(lefts)
    return pl.pallas_call(
        functools.partial(grad_kernel, count),
        out_shape=(jax.ShapeDtypeStruct((units, width), jnp.bfloat16),) * count,
        in_specs=[VMEM] * (count + 1),
        out_specs=(HBM,) * count,
        scratch_shapes=[
            pltpu.VMEM((count, units, width), jnp.bfloat16),
            pltpu.SemaphoreType.DMA((count, pl.cdiv(width, CHUNK))),
        ],
        compiler_params=pltpu.CompilerParams(vmem_limit_bytes=24 << 20),
        cost_estimate=pl.CostEstimate(
            flops=2 * total * units * width * count,
            bytes_accessed=units * width * 4 * count,
            transcendentals=0,
        ),
        name="weight_grads",
    )(*lefts, rows)


def expand_kernel(kept_ref, *refs):
    homes, out_ref = refs[:-1], refs[-1]
    tokens, width = out_ref.shape
    combined = kept_ref[:, :width]
    for home in homes:
        combined = combined + home[...].astype(jnp.float32)
    numbers = kept_ref[:, width : width + 1]
    column = lax.broadcasted_iota(jnp.int32, (CAP, tokens), 1).astype(jnp.float32)
    chooser = jnp.where(column == numbers, 1.0, 0.0).astype(jnp.bfloat16)
    out_ref[...] = contract_first(chooser, combined.astype(jnp.bfloat16)).astype(jnp.bfloat16)


def expand(kept, homes, tokens, width):
    return pl.pallas_call(
        expand_kernel,
        out_shape=jax.ShapeDtypeStruct((tokens, width), jnp.bfloat16),
        in_specs=[VMEM] * (len(homes) + 1),
        out_specs=VMEM,
        compiler_params=pltpu.CompilerParams(vmem_limit_bytes=8 << 20),
        name="expand",
    )(kept, *homes)


def swap(value, bits):
    peers = lax.axis_size("expert")
    return lax.ppermute(value, "expert", [(i, i ^ bits) for i in range(peers)])


def shift_back(value, bits):
    count, peers = lax.axis_size("pipe"), lax.axis_size("expert")
    pairs = [
        (section * peers + i, (section - 1) * peers + (i ^ bits))
        for section in range(1, count)
        for i in range(peers)
    ]
    return lax.ppermute(value, ("pipe", "expert"), pairs)


def one_expert(own, slots, weights, tokens, width):
    weights = fetch(own, *weights)
    first, second, third = (swap(own, bits) for bits in OUT)
    across = [swap(jnp.concatenate([own, first, second], axis=0), 1)]
    across.append(swap(third, 1))
    pieces = (own, first, second, third, *across)
    rows, gate, up, hidden, keep, send = expert_main(pieces, slots, *weights, split=True)
    beside, kept = shift_back(send, 1), shift_back(keep, 0)
    grads = weight_grads(rows, gate, up, hidden)
    kept = kept.astype(jnp.float32)
    summed = kept[:, :width] + beside.astype(jnp.float32)
    rounded = summed.astype(jnp.bfloat16)
    homes = [
        swap(rounded[(OUT.index(bits) + 1) * CAP : (OUT.index(bits) + 2) * CAP], bits)
        for bits in HOME
    ]
    kept = jnp.concatenate([summed[:CAP], kept[:CAP, width:]], axis=1)
    return grads, expand(kept, homes, tokens, width)


def many_experts(own, slots, weights, ids, peers, flight, tokens, width):
    spread = jnp.repeat(own.reshape(flight, PAIR, width), SLICES, axis=0)
    received = lax.all_to_all(spread, "expert", split_axis=0, concat_axis=0, tiled=True)
    received = received.reshape(peers * PAIR, width)
    rows, gate, up, hidden, partial = expert_main((received,), slots, *weights, split=False)
    partial = partial.reshape(peers, CAP, width)
    returned = lax.all_to_all(partial, "expert", split_axis=0, concat_axis=0, tiled=True)
    grads = weight_grads(rows, gate, up, hidden)
    combined = jnp.sum(
        returned.astype(jnp.float32).reshape(flight, SLICES, CAP, width), axis=1
    ).reshape(flight * CAP, width)
    labels = jnp.arange(flight, dtype=jnp.int32)
    named = jnp.any(ids[None] == labels[:, None, None], axis=1)
    ranks = jnp.cumsum(named.astype(jnp.int32), axis=1) - 1
    slot = jnp.arange(CAP, dtype=jnp.int32)
    chooser = named[:, None, :] & (ranks[:, None, :] == slot[None, :, None])
    chooser = chooser.reshape(flight * CAP, tokens).astype(jnp.float32)
    input_grad = lax.dot_general(
        chooser,
        combined,
        (((0,), (0,)), ((), ())),
        precision=lax.Precision.HIGHEST,
        preferred_element_type=jnp.float32,
    )
    return grads, shift_back(input_grad.astype(jnp.bfloat16), 0)


def body(layer_input, grad_output, expert_ids, gate_probs, w_gate, w_up, w_down):
    peers = lax.axis_size("expert")
    flight = peers // SLICES
    tokens, width = layer_input.shape[1:]
    ids = expert_ids[0].T
    weights = (w_gate[0], w_up[0], w_down[0])
    own, slots = select_rows(ids, gate_probs[0].T, layer_input[0], grad_output[0], flight)
    if flight == 1:
        grads, shifted = one_expert(own, slots, weights, tokens, width)
    else:
        grads, shifted = many_experts(
            own, slots, weights, ids, peers, flight, tokens, width
        )
    return tuple(grad[None] for grad in grads) + (shifted[None],)


def solution(mesh):
    spec = P("pipe", "expert", None)
    return jax.shard_map(
        body, mesh=mesh, in_specs=(spec,) * 7, out_specs=(spec,) * 4, check_vma=False
    )
```

```python
import functools

import jax
import jax.numpy as jnp
from jax import lax
from jax.experimental import pallas as pl
from jax.experimental.pallas import tpu as pltpu
from jax.sharding import PartitionSpec as P


SLICES = 8
CAP = 4
PAIR = 2 * CAP
LANES = 128
CHUNK = 1024
OUT = (4, 2, 6)
HOME = (4, 6, 2)

VMEM = pl.BlockSpec(memory_space=pltpu.VMEM)
HBM = pl.BlockSpec(memory_space=pl.ANY)


def contract_last(left, right):
    return lax.dot_general(
        left, right, (((1,), (1,)), ((), ())), preferred_element_type=jnp.float32
    )


def contract_first(left, right):
    return lax.dot_general(
        left, right, (((0,), (0,)), ((), ())), preferred_element_type=jnp.float32
    )


def select_kernel(flight, *refs):
    routes_ref, sources = refs[0], refs[1:3]
    (rows_ref, slots_ref), held, sems = refs[3:5], refs[5:7], refs[7]
    copies = [
        pltpu.make_async_copy(source, target, sems.at[i])
        for i, (source, target) in enumerate(zip(sources, held))
    ]
    for copy in copies:
        copy.start()
    tokens = routes_ref.shape[2]
    before = lax.broadcasted_iota(jnp.int32, (tokens, tokens), 0) < lax.broadcasted_iota(
        jnp.int32, (tokens, tokens), 1
    )
    before = before.astype(jnp.float32).astype(jnp.bfloat16)
    row = lax.broadcasted_iota(jnp.int32, (PAIR, tokens), 0)
    token = lax.broadcasted_iota(jnp.int32, (PAIR, tokens), 1).astype(jnp.float32)
    slot = lax.rem(row, CAP)
    choosers = []
    for expert in range(flight):
        prob = jnp.sum(routes_ref[expert], axis=0, keepdims=True)
        hits = jnp.broadcast_to(jnp.where(prob > 0.0, 1.0, 0.0), (PAIR, tokens))
        ranks = jnp.dot(hits.astype(jnp.bfloat16), before, preferred_element_type=jnp.float32)
        chosen = jnp.where((hits > 0.5) & (ranks.astype(jnp.int32) == slot), 1.0, 0.0)
        scale = jnp.sum(chosen * prob, axis=1, keepdims=True)
        number = jnp.sum(chosen * token, axis=1, keepdims=True)
        slots_ref[pl.ds(expert * PAIR, PAIR), :] = jnp.broadcast_to(number, (PAIR, LANES))
        choosers.append((chosen.astype(jnp.bfloat16), scale))
    for copy in copies:
        copy.wait()
    for expert, (chooser, scale) in enumerate(choosers):
        taken = jnp.dot(chooser, held[0][...], preferred_element_type=jnp.float32)
        cotan = jnp.dot(chooser, held[1][...], preferred_element_type=jnp.float32) * scale
        wide = lax.broadcasted_iota(jnp.int32, taken.shape, 0) < CAP
        rows_ref[pl.ds(expert * PAIR, PAIR), :] = jnp.where(wide, taken, cotan).astype(
            jnp.bfloat16
        )


def select_rows(ids, probs, inputs, cotan, flight):
    width = inputs.shape[1]
    labels = jnp.arange(flight, dtype=jnp.int32)
    routes = jnp.where(ids[None] == labels[:, None, None], probs[None], 0.0)
    return pl.pallas_call(
        functools.partial(select_kernel, flight),
        out_shape=(
            jax.ShapeDtypeStruct((flight * PAIR, width), jnp.bfloat16),
            jax.ShapeDtypeStruct((flight * PAIR, LANES), jnp.float32),
        ),
        in_specs=[VMEM, HBM, HBM],
        out_specs=(VMEM, VMEM),
        scratch_shapes=[pltpu.VMEM(value.shape, value.dtype) for value in (inputs, cotan)]
        + [pltpu.SemaphoreType.DMA((2,))],
        compiler_params=pltpu.CompilerParams(vmem_limit_bytes=55000 << 10),
        name="select",
    )(routes, inputs, cotan)


def join_kernel(*refs):
    out_ref, start = refs[-1], 0
    for ref in refs[:-1]:
        out_ref[pl.ds(start, ref.shape[0]), :] = ref[...]
        start += ref.shape[0]


def join(*pieces):
    rows, width = sum(piece.shape[0] for piece in pieces), pieces[0].shape[1]
    return pl.pallas_call(
        join_kernel,
        out_shape=jax.ShapeDtypeStruct((rows, width), pieces[0].dtype),
        in_specs=[VMEM] * len(pieces),
        out_specs=VMEM,
        compiler_params=pltpu.CompilerParams(vmem_limit_bytes=1 << 20),
        cost_estimate=pl.CostEstimate(flops=10**10, bytes_accessed=0, transcendentals=0),
        name="join",
    )(*pieces)


def main_kernel(pieces, split, *refs):
    row_refs, refs = refs[:pieces], refs[pieces:]
    slots_ref, gate_ref, up_ref, down_ref = refs[:4]
    all_ref, gate_out, up_out, hidden_out = refs[4:8]
    partial_refs = refs[8:]
    start = 0
    for ref in row_refs:
        all_ref[pl.ds(start, ref.shape[0]), :] = ref[...]
        start += ref.shape[0]
    rows = all_ref[...]
    total = rows.shape[0]
    pre_gate = contract_last(rows, gate_ref[...])
    pre_up = contract_last(rows, up_ref[...])
    hidden_grad = pltpu.roll(contract_last(rows, down_ref[...]), total - CAP, 0)
    sigma = jax.nn.sigmoid(pre_gate)
    silu_val = pre_gate * sigma
    silu_grad = sigma * (1.0 + pre_gate * (1.0 - sigma))
    first = lax.rem(lax.broadcasted_iota(jnp.int32, pre_gate.shape, 0), PAIR) < CAP
    hidden = jnp.where(first, silu_val * pre_up, 0.0)
    grad_gate = jnp.where(first, hidden_grad * pre_up * silu_grad, 0.0)
    grad_up = jnp.where(first, hidden_grad * silu_val, 0.0)
    gate_out[...] = grad_gate.astype(jnp.bfloat16)
    up_out[...] = grad_up.astype(jnp.bfloat16)
    hidden_out[...] = pltpu.roll(hidden, CAP, 0).astype(jnp.bfloat16)

    def packed(value):
        blocks = total // PAIR
        moved = pltpu.roll(value, CAP, 0)
        return jnp.concatenate(
            [
                value[2 * m * PAIR : (2 * m + 1) * PAIR]
                + moved[(2 * m + 1) * PAIR : (2 * m + 2) * PAIR]
                for m in range(blocks // 2)
            ],
            axis=0,
        ).astype(jnp.bfloat16)

    partial = jnp.dot(packed(grad_gate), gate_ref[...], preferred_element_type=jnp.float32)
    partial = partial + jnp.dot(
        packed(grad_up), up_ref[...], preferred_element_type=jnp.float32
    )
    if split:
        half, width = partial.shape[0] // 2, partial.shape[1]
        keep_ref, send_ref = partial_refs
        send_ref[...] = partial[half:].astype(jnp.bfloat16)
        keep_ref[:, :width] = partial[:half].astype(jnp.bfloat16)
        keep_ref[:PAIR, width:] = slots_ref[...].astype(jnp.bfloat16)
        keep_ref[PAIR:, width:] = jnp.zeros((half - PAIR, LANES), jnp.bfloat16)
    else:
        partial_refs[0][...] = partial.astype(jnp.bfloat16)


def expert_main(pieces, slots, weight_gate, weight_up, weight_down, split):
    total = sum(piece.shape[0] for piece in pieces)
    units, width = weight_gate.shape
    rows = total // 2
    small = jax.ShapeDtypeStruct((total, units), jnp.bfloat16)
    if split:
        partials = (
            jax.ShapeDtypeStruct((rows // 2, width + LANES), jnp.bfloat16),
            jax.ShapeDtypeStruct((rows // 2, width), jnp.bfloat16),
        )
    else:
        partials = (jax.ShapeDtypeStruct((rows, width), jnp.bfloat16),)
    outs = (jax.ShapeDtypeStruct((total, width), jnp.bfloat16), small, small, small) + partials
    return pl.pallas_call(
        functools.partial(main_kernel, len(pieces), split),
        out_shape=outs,
        in_specs=[VMEM] * (len(pieces) + 4),
        out_specs=(VMEM,) * len(outs),
        compiler_params=pltpu.CompilerParams(vmem_limit_bytes=32 << 20),
        cost_estimate=pl.CostEstimate(
            flops=2 * total * units * width * 5,
            bytes_accessed=3 * units * width * 2,
            transcendentals=total * units,
        ),
        name="expert_main",
    )(*pieces, slots, weight_gate, weight_up, weight_down)


def grad_kernel(count, *refs):
    lefts, rows_ref, outs = refs[:count], refs[count], refs[count + 1 : 2 * count + 1]
    held_ref, sems = refs[2 * count + 1 :]
    width = rows_ref.shape[1]
    copies = []
    for j in range(count):
        left = lefts[j][...]
        for c, start in enumerate(range(0, width, CHUNK)):
            part = pl.ds(start, min(CHUNK, width - start))
            held_ref[j, :, part] = contract_first(left, rows_ref[:, part]).astype(jnp.bfloat16)
            copy = pltpu.make_async_copy(
                held_ref.at[j, :, part], outs[j].at[:, part], sems.at[j, c]
            )
            copy.start()
            copies.append(copy)
    for copy in copies:
        copy.wait()


def weight_grads(rows, *lefts):
    total, width = rows.shape
    units = lefts[0].shape[1]
    count = len(lefts)
    return pl.pallas_call(
        functools.partial(grad_kernel, count),
        out_shape=(jax.ShapeDtypeStruct((units, width), jnp.bfloat16),) * count,
        in_specs=[VMEM] * (count + 1),
        out_specs=(HBM,) * count,
        scratch_shapes=[
            pltpu.VMEM((count, units, width), jnp.bfloat16),
            pltpu.SemaphoreType.DMA((count, pl.cdiv(width, CHUNK))),
        ],
        compiler_params=pltpu.CompilerParams(vmem_limit_bytes=24 << 20),
        cost_estimate=pl.CostEstimate(
            flops=2 * total * units * width * count,
            bytes_accessed=units * width * 4 * count,
            transcendentals=0,
        ),
        name="weight_grads",
    )(*lefts, rows)


def expand_kernel(kept_ref, *refs):
    homes, out_ref = refs[:-1], refs[-1]
    tokens, width = out_ref.shape
    combined = kept_ref[:, :width]
    for home in homes:
        combined = combined + home[...].astype(jnp.float32)
    numbers = kept_ref[:, width : width + 1]
    column = lax.broadcasted_iota(jnp.int32, (CAP, tokens), 1).astype(jnp.float32)
    chooser = jnp.where(column == numbers, 1.0, 0.0).astype(jnp.bfloat16)
    out_ref[...] = contract_first(chooser, combined.astype(jnp.bfloat16)).astype(jnp.bfloat16)


def expand(kept, homes, tokens, width):
    return pl.pallas_call(
        expand_kernel,
        out_shape=jax.ShapeDtypeStruct((tokens, width), jnp.bfloat16),
        in_specs=[VMEM] * (len(homes) + 1),
        out_specs=VMEM,
        compiler_params=pltpu.CompilerParams(vmem_limit_bytes=8 << 20),
        name="expand",
    )(kept, *homes)


def swap(value, bits):
    peers = lax.axis_size("expert")
    return lax.ppermute(value, "expert", [(i, i ^ bits) for i in range(peers)])


def shift_back(value, bits):
    count, peers = lax.axis_size("pipe"), lax.axis_size("expert")
    pairs = [
        (section * peers + i, (section - 1) * peers + (i ^ bits))
        for section in range(1, count)
        for i in range(peers)
    ]
    return lax.ppermute(value, ("pipe", "expert"), pairs)


def one_expert(own, slots, weights, tokens, width):
    first, second, third = (swap(own, bits) for bits in OUT)
    across = [swap(join(own, first, second), 1)]
    across.append(swap(third, 1))
    pieces = (own, first, second, third, *across)
    rows, gate, up, hidden, keep, send = expert_main(pieces, slots, *weights, split=True)
    beside, kept = shift_back(send, 1), shift_back(keep, 0)
    grads = weight_grads(rows, gate, up, hidden)
    kept = kept.astype(jnp.float32)
    summed = kept[:, :width] + beside.astype(jnp.float32)
    rounded = summed.astype(jnp.bfloat16)
    homes = [
        swap(rounded[(OUT.index(bits) + 1) * CAP : (OUT.index(bits) + 2) * CAP], bits)
        for bits in HOME
    ]
    kept = jnp.concatenate([summed[:CAP], kept[:CAP, width:]], axis=1)
    return grads, expand(kept, homes, tokens, width)


def many_experts(own, slots, weights, ids, peers, flight, tokens, width):
    spread = jnp.repeat(own.reshape(flight, PAIR, width), SLICES, axis=0)
    received = lax.all_to_all(spread, "expert", split_axis=0, concat_axis=0, tiled=True)
    received = received.reshape(peers * PAIR, width)
    rows, gate, up, hidden, partial = expert_main((received,), slots, *weights, split=False)
    partial = partial.reshape(peers, CAP, width)
    returned = lax.all_to_all(partial, "expert", split_axis=0, concat_axis=0, tiled=True)
    grads = weight_grads(rows, gate, up, hidden)
    combined = jnp.sum(
        returned.astype(jnp.float32).reshape(flight, SLICES, CAP, width), axis=1
    ).reshape(flight * CAP, width)
    labels = jnp.arange(flight, dtype=jnp.int32)
    named = jnp.any(ids[None] == labels[:, None, None], axis=1)
    ranks = jnp.cumsum(named.astype(jnp.int32), axis=1) - 1
    slot = jnp.arange(CAP, dtype=jnp.int32)
    chooser = named[:, None, :] & (ranks[:, None, :] == slot[None, :, None])
    chooser = chooser.reshape(flight * CAP, tokens).astype(jnp.float32)
    input_grad = lax.dot_general(
        chooser,
        combined,
        (((0,), (0,)), ((), ())),
        precision=lax.Precision.HIGHEST,
        preferred_element_type=jnp.float32,
    )
    return grads, shift_back(input_grad.astype(jnp.bfloat16), 0)


def body(layer_input, grad_output, expert_ids, gate_probs, w_gate, w_up, w_down):
    peers = lax.axis_size("expert")
    flight = peers // SLICES
    tokens, width = layer_input.shape[1:]
    ids = expert_ids[0].T
    weights = (w_gate[0], w_up[0], w_down[0])
    own, slots = select_rows(ids, gate_probs[0].T, layer_input[0], grad_output[0], flight)
    if flight == 1:
        grads, shifted = one_expert(own, slots, weights, tokens, width)
    else:
        grads, shifted = many_experts(
            own, slots, weights, ids, peers, flight, tokens, width
        )
    return tuple(grad[None] for grad in grads) + (shifted[None],)


def solution(mesh):
    spec = P("pipe", "expert", None)
    return jax.shard_map(
        body, mesh=mesh, in_specs=(spec,) * 7, out_specs=(spec,) * 4, check_vma=False
    )
```

```python
import functools

import jax
import jax.numpy as jnp
from jax import lax
from jax.experimental import pallas as pl
from jax.experimental.pallas import tpu as pltpu
from jax.sharding import PartitionSpec as P


SLICES = 8
CAP = 4
PAIR = 2 * CAP
LANES = 128
CHUNK = 1024
OUT = (4, 2, 6)
HOME = (4, 6, 2)

VMEM = pl.BlockSpec(memory_space=pltpu.VMEM)
HBM = pl.BlockSpec(memory_space=pl.ANY)


def contract_last(left, right):
    return lax.dot_general(
        left, right, (((1,), (1,)), ((), ())), preferred_element_type=jnp.float32
    )


def contract_first(left, right):
    return lax.dot_general(
        left, right, (((0,), (0,)), ((), ())), preferred_element_type=jnp.float32
    )


def route_kernel(flight, routes_ref, chooser_ref, scale_ref, slots_ref):
    tokens = routes_ref.shape[2]
    before = lax.broadcasted_iota(jnp.int32, (tokens, tokens), 0) < lax.broadcasted_iota(
        jnp.int32, (tokens, tokens), 1
    )
    before = before.astype(jnp.float32).astype(jnp.bfloat16)
    row = lax.broadcasted_iota(jnp.int32, (PAIR, tokens), 0)
    token = lax.broadcasted_iota(jnp.int32, (PAIR, tokens), 1).astype(jnp.float32)
    slot = lax.rem(row, CAP)
    for expert in range(flight):
        prob = jnp.sum(routes_ref[expert], axis=0, keepdims=True)
        hits = jnp.broadcast_to(jnp.where(prob > 0.0, 1.0, 0.0), (PAIR, tokens))
        ranks = jnp.dot(hits.astype(jnp.bfloat16), before, preferred_element_type=jnp.float32)
        chosen = jnp.where((hits > 0.5) & (ranks.astype(jnp.int32) == slot), 1.0, 0.0)
        scale = jnp.sum(chosen * prob, axis=1, keepdims=True)
        number = jnp.sum(chosen * token, axis=1, keepdims=True)
        part = pl.ds(expert * PAIR, PAIR)
        slots_ref[part, :] = jnp.broadcast_to(number, (PAIR, LANES))
        scale_ref[part, :] = jnp.broadcast_to(scale, (PAIR, LANES))
        chooser_ref[part, :] = chosen.astype(jnp.bfloat16)


def select_kernel(chooser_ref, scale_ref, input_ref, cotan_ref, rows_ref):
    for start in range(0, rows_ref.shape[0], PAIR):
        part = pl.ds(start, PAIR)
        chooser = chooser_ref[part, :]
        taken = jnp.dot(chooser, input_ref[...], preferred_element_type=jnp.float32)
        cotan = jnp.dot(chooser, cotan_ref[...], preferred_element_type=jnp.float32)
        wide = lax.broadcasted_iota(jnp.int32, taken.shape, 0) < CAP
        rows_ref[part, :] = jnp.where(wide, taken, cotan * scale_ref[part, :1]).astype(
            jnp.bfloat16
        )


def select_rows(ids, probs, inputs, cotan, flight):
    width = inputs.shape[1]
    labels = jnp.arange(flight, dtype=jnp.int32)
    routes = jnp.where(ids[None] == labels[:, None, None], probs[None], 0.0)
    rows = flight * PAIR
    chooser, scale, slots = pl.pallas_call(
        functools.partial(route_kernel, flight),
        out_shape=(
            jax.ShapeDtypeStruct((rows, ids.shape[1]), jnp.bfloat16),
            jax.ShapeDtypeStruct((rows, LANES), jnp.float32),
            jax.ShapeDtypeStruct((rows, LANES), jnp.float32),
        ),
        in_specs=[VMEM],
        out_specs=(VMEM,) * 3,
        compiler_params=pltpu.CompilerParams(vmem_limit_bytes=2 << 20),
        cost_estimate=pl.CostEstimate(flops=10**9, bytes_accessed=0, transcendentals=0),
        name="route",
    )(routes)
    taken = pl.pallas_call(
        select_kernel,
        out_shape=jax.ShapeDtypeStruct((rows, width), jnp.bfloat16),
        in_specs=[VMEM] * 4,
        out_specs=VMEM,
        compiler_params=pltpu.CompilerParams(vmem_limit_bytes=2 << 20),
        name="select",
    )(chooser, scale, inputs, cotan)
    return taken, slots


def join_kernel(*refs):
    out_ref, start = refs[-1], 0
    for ref in refs[:-1]:
        out_ref[pl.ds(start, ref.shape[0]), :] = ref[...]
        start += ref.shape[0]


def join(*pieces):
    rows, width = sum(piece.shape[0] for piece in pieces), pieces[0].shape[1]
    return pl.pallas_call(
        join_kernel,
        out_shape=jax.ShapeDtypeStruct((rows, width), pieces[0].dtype),
        in_specs=[VMEM] * len(pieces),
        out_specs=VMEM,
        compiler_params=pltpu.CompilerParams(vmem_limit_bytes=1 << 20),
        cost_estimate=pl.CostEstimate(flops=10**10, bytes_accessed=0, transcendentals=0),
        name="join",
    )(*pieces)


def main_kernel(pieces, split, *refs):
    row_refs, refs = refs[:pieces], refs[pieces:]
    slots_ref, gate_ref, up_ref, down_ref = refs[:4]
    all_ref, gate_out, up_out, hidden_out = refs[4:8]
    partial_refs = refs[8:]
    start = 0
    for ref in row_refs:
        all_ref[pl.ds(start, ref.shape[0]), :] = ref[...]
        start += ref.shape[0]
    rows = all_ref[...]
    total = rows.shape[0]
    pre_gate = contract_last(rows, gate_ref[...])
    pre_up = contract_last(rows, up_ref[...])
    hidden_grad = pltpu.roll(contract_last(rows, down_ref[...]), total - CAP, 0)
    sigma = jax.nn.sigmoid(pre_gate)
    silu_val = pre_gate * sigma
    silu_grad = sigma * (1.0 + pre_gate * (1.0 - sigma))
    first = lax.rem(lax.broadcasted_iota(jnp.int32, pre_gate.shape, 0), PAIR) < CAP
    hidden = jnp.where(first, silu_val * pre_up, 0.0)
    grad_gate = jnp.where(first, hidden_grad * pre_up * silu_grad, 0.0)
    grad_up = jnp.where(first, hidden_grad * silu_val, 0.0)
    gate_out[...] = grad_gate.astype(jnp.bfloat16)
    up_out[...] = grad_up.astype(jnp.bfloat16)
    hidden_out[...] = pltpu.roll(hidden, CAP, 0).astype(jnp.bfloat16)

    def packed(value):
        blocks = total // PAIR
        moved = pltpu.roll(value, CAP, 0)
        return jnp.concatenate(
            [
                value[2 * m * PAIR : (2 * m + 1) * PAIR]
                + moved[(2 * m + 1) * PAIR : (2 * m + 2) * PAIR]
                for m in range(blocks // 2)
            ],
            axis=0,
        ).astype(jnp.bfloat16)

    partial = jnp.dot(packed(grad_gate), gate_ref[...], preferred_element_type=jnp.float32)
    partial = partial + jnp.dot(
        packed(grad_up), up_ref[...], preferred_element_type=jnp.float32
    )
    if split:
        half, width = partial.shape[0] // 2, partial.shape[1]
        keep_ref, send_ref = partial_refs
        send_ref[...] = partial[half:].astype(jnp.bfloat16)
        keep_ref[:, :width] = partial[:half].astype(jnp.bfloat16)
        keep_ref[:PAIR, width:] = slots_ref[...].astype(jnp.bfloat16)
        keep_ref[PAIR:, width:] = jnp.zeros((half - PAIR, LANES), jnp.bfloat16)
    else:
        partial_refs[0][...] = partial.astype(jnp.bfloat16)


def expert_main(pieces, slots, weight_gate, weight_up, weight_down, split):
    total = sum(piece.shape[0] for piece in pieces)
    units, width = weight_gate.shape
    rows = total // 2
    small = jax.ShapeDtypeStruct((total, units), jnp.bfloat16)
    if split:
        partials = (
            jax.ShapeDtypeStruct((rows // 2, width + LANES), jnp.bfloat16),
            jax.ShapeDtypeStruct((rows // 2, width), jnp.bfloat16),
        )
    else:
        partials = (jax.ShapeDtypeStruct((rows, width), jnp.bfloat16),)
    outs = (jax.ShapeDtypeStruct((total, width), jnp.bfloat16), small, small, small) + partials
    return pl.pallas_call(
        functools.partial(main_kernel, len(pieces), split),
        out_shape=outs,
        in_specs=[VMEM] * (len(pieces) + 4),
        out_specs=(VMEM,) * len(outs),
        compiler_params=pltpu.CompilerParams(vmem_limit_bytes=32 << 20),
        cost_estimate=pl.CostEstimate(
            flops=2 * total * units * width * 5,
            bytes_accessed=3 * units * width * 2,
            transcendentals=total * units,
        ),
        name="expert_main",
    )(*pieces, slots, weight_gate, weight_up, weight_down)


def grad_kernel(count, *refs):
    lefts, rows_ref, outs = refs[:count], refs[count], refs[count + 1 : 2 * count + 1]
    held_ref, sems = refs[2 * count + 1 :]
    width = rows_ref.shape[1]
    copies = []
    for j in range(count):
        left = lefts[j][...]
        for c, start in enumerate(range(0, width, CHUNK)):
            part = pl.ds(start, min(CHUNK, width - start))
            held_ref[j, :, part] = contract_first(left, rows_ref[:, part]).astype(jnp.bfloat16)
            copy = pltpu.make_async_copy(
                held_ref.at[j, :, part], outs[j].at[:, part], sems.at[j, c]
            )
            copy.start()
            copies.append(copy)
    for copy in copies:
        copy.wait()


def weight_grads(rows, *lefts):
    total, width = rows.shape
    units = lefts[0].shape[1]
    count = len(lefts)
    return pl.pallas_call(
        functools.partial(grad_kernel, count),
        out_shape=(jax.ShapeDtypeStruct((units, width), jnp.bfloat16),) * count,
        in_specs=[VMEM] * (count + 1),
        out_specs=(HBM,) * count,
        scratch_shapes=[
            pltpu.VMEM((count, units, width), jnp.bfloat16),
            pltpu.SemaphoreType.DMA((count, pl.cdiv(width, CHUNK))),
        ],
        compiler_params=pltpu.CompilerParams(vmem_limit_bytes=24 << 20),
        cost_estimate=pl.CostEstimate(
            flops=2 * total * units * width * count,
            bytes_accessed=units * width * 4 * count,
            transcendentals=0,
        ),
        name="weight_grads",
    )(*lefts, rows)


def expand_kernel(kept_ref, *refs):
    homes, out_ref = refs[:-1], refs[-1]
    tokens, width = out_ref.shape
    combined = kept_ref[:, :width]
    for home in homes:
        combined = combined + home[...].astype(jnp.float32)
    numbers = kept_ref[:, width : width + 1]
    column = lax.broadcasted_iota(jnp.int32, (CAP, tokens), 1).astype(jnp.float32)
    chooser = jnp.where(column == numbers, 1.0, 0.0).astype(jnp.bfloat16)
    out_ref[...] = contract_first(chooser, combined.astype(jnp.bfloat16)).astype(jnp.bfloat16)


def expand(kept, homes, tokens, width):
    return pl.pallas_call(
        expand_kernel,
        out_shape=jax.ShapeDtypeStruct((tokens, width), jnp.bfloat16),
        in_specs=[VMEM] * (len(homes) + 1),
        out_specs=VMEM,
        compiler_params=pltpu.CompilerParams(vmem_limit_bytes=8 << 20),
        name="expand",
    )(kept, *homes)


def swap(value, bits):
    peers = lax.axis_size("expert")
    return lax.ppermute(value, "expert", [(i, i ^ bits) for i in range(peers)])


def shift_back(value, bits):
    count, peers = lax.axis_size("pipe"), lax.axis_size("expert")
    pairs = [
        (section * peers + i, (section - 1) * peers + (i ^ bits))
        for section in range(1, count)
        for i in range(peers)
    ]
    return lax.ppermute(value, ("pipe", "expert"), pairs)


def one_expert(own, slots, weights, tokens, width):
    first, second, third = (swap(own, bits) for bits in OUT)
    across = [swap(join(own, first, second), 1)]
    across.append(swap(third, 1))
    pieces = (own, first, second, third, *across)
    rows, gate, up, hidden, keep, send = expert_main(pieces, slots, *weights, split=True)
    beside, kept = shift_back(send, 1), shift_back(keep, 0)
    grads = weight_grads(rows, gate, up, hidden)
    kept = kept.astype(jnp.float32)
    summed = kept[:, :width] + beside.astype(jnp.float32)
    rounded = summed.astype(jnp.bfloat16)
    homes = [
        swap(rounded[(OUT.index(bits) + 1) * CAP : (OUT.index(bits) + 2) * CAP], bits)
        for bits in HOME
    ]
    kept = jnp.concatenate([summed[:CAP], kept[:CAP, width:]], axis=1)
    return grads, expand(kept, homes, tokens, width)


def many_experts(own, slots, weights, ids, peers, flight, tokens, width):
    spread = jnp.repeat(own.reshape(flight, PAIR, width), SLICES, axis=0)
    received = lax.all_to_all(spread, "expert", split_axis=0, concat_axis=0, tiled=True)
    received = received.reshape(peers * PAIR, width)
    rows, gate, up, hidden, partial = expert_main((received,), slots, *weights, split=False)
    partial = partial.reshape(peers, CAP, width)
    returned = lax.all_to_all(partial, "expert", split_axis=0, concat_axis=0, tiled=True)
    grads = weight_grads(rows, gate, up, hidden)
    combined = jnp.sum(
        returned.astype(jnp.float32).reshape(flight, SLICES, CAP, width), axis=1
    ).reshape(flight * CAP, width)
    labels = jnp.arange(flight, dtype=jnp.int32)
    named = jnp.any(ids[None] == labels[:, None, None], axis=1)
    ranks = jnp.cumsum(named.astype(jnp.int32), axis=1) - 1
    slot = jnp.arange(CAP, dtype=jnp.int32)
    chooser = named[:, None, :] & (ranks[:, None, :] == slot[None, :, None])
    chooser = chooser.reshape(flight * CAP, tokens).astype(jnp.float32)
    input_grad = lax.dot_general(
        chooser,
        combined,
        (((0,), (0,)), ((), ())),
        precision=lax.Precision.HIGHEST,
        preferred_element_type=jnp.float32,
    )
    return grads, shift_back(input_grad.astype(jnp.bfloat16), 0)


def body(layer_input, grad_output, expert_ids, gate_probs, w_gate, w_up, w_down):
    peers = lax.axis_size("expert")
    flight = peers // SLICES
    tokens, width = layer_input.shape[1:]
    ids = expert_ids[0].T
    weights = (w_gate[0], w_up[0], w_down[0])
    own, slots = select_rows(ids, gate_probs[0].T, layer_input[0], grad_output[0], flight)
    if flight == 1:
        grads, shifted = one_expert(own, slots, weights, tokens, width)
    else:
        grads, shifted = many_experts(
            own, slots, weights, ids, peers, flight, tokens, width
        )
    return tuple(grad[None] for grad in grads) + (shifted[None],)


def solution(mesh):
    spec = P("pipe", "expert", None)
    return jax.shard_map(
        body, mesh=mesh, in_specs=(spec,) * 7, out_specs=(spec,) * 4, check_vma=False
    )
```

```python
import functools

import jax
import jax.numpy as jnp
from jax import lax
from jax.experimental import pallas as pl
from jax.experimental.pallas import tpu as pltpu
from jax.sharding import PartitionSpec as P


SLICES = 8
CAP = 4
PAIR = 2 * CAP
LANES = 128
CHUNK = 1024
UNIT_CHUNK = 256
WIDTH_CHUNK = 1536
OUT = (4, 2, 6)
HOME = (4, 6, 2)

VMEM = pl.BlockSpec(memory_space=pltpu.VMEM)
HBM = pl.BlockSpec(memory_space=pl.ANY)


def contract_last(left, right):
    return lax.dot_general(
        left, right, (((1,), (1,)), ((), ())), preferred_element_type=jnp.float32
    )


def contract_first(left, right):
    return lax.dot_general(
        left, right, (((0,), (0,)), ((), ())), preferred_element_type=jnp.float32
    )


def route_kernel(flight, routes_ref, chooser_ref, scale_ref, slots_ref):
    tokens = routes_ref.shape[2]
    before = lax.broadcasted_iota(jnp.int32, (tokens, tokens), 0) < lax.broadcasted_iota(
        jnp.int32, (tokens, tokens), 1
    )
    before = before.astype(jnp.float32).astype(jnp.bfloat16)
    row = lax.broadcasted_iota(jnp.int32, (PAIR, tokens), 0)
    token = lax.broadcasted_iota(jnp.int32, (PAIR, tokens), 1).astype(jnp.float32)
    slot = lax.rem(row, CAP)
    for expert in range(flight):
        prob = jnp.sum(routes_ref[expert], axis=0, keepdims=True)
        hits = jnp.broadcast_to(jnp.where(prob > 0.0, 1.0, 0.0), (PAIR, tokens))
        ranks = jnp.dot(hits.astype(jnp.bfloat16), before, preferred_element_type=jnp.float32)
        chosen = jnp.where((hits > 0.5) & (ranks.astype(jnp.int32) == slot), 1.0, 0.0)
        scale = jnp.sum(chosen * prob, axis=1, keepdims=True)
        number = jnp.sum(chosen * token, axis=1, keepdims=True)
        part = pl.ds(expert * PAIR, PAIR)
        slots_ref[part, :] = jnp.broadcast_to(number, (PAIR, LANES))
        scale_ref[part, :] = jnp.broadcast_to(scale, (PAIR, LANES))
        chooser_ref[part, :] = chosen.astype(jnp.bfloat16)


def select_kernel(chooser_ref, scale_ref, input_ref, cotan_ref, rows_ref):
    for start in range(0, rows_ref.shape[0], PAIR):
        part = pl.ds(start, PAIR)
        chooser = chooser_ref[part, :]
        taken = jnp.dot(chooser, input_ref[...], preferred_element_type=jnp.float32)
        cotan = jnp.dot(chooser, cotan_ref[...], preferred_element_type=jnp.float32)
        wide = lax.broadcasted_iota(jnp.int32, taken.shape, 0) < CAP
        rows_ref[part, :] = jnp.where(wide, taken, cotan * scale_ref[part, :1]).astype(
            jnp.bfloat16
        )


def select_rows(ids, probs, inputs, cotan, flight):
    width = inputs.shape[1]
    labels = jnp.arange(flight, dtype=jnp.int32)
    routes = jnp.where(ids[None] == labels[:, None, None], probs[None], 0.0)
    rows = flight * PAIR
    chooser, scale, slots = pl.pallas_call(
        functools.partial(route_kernel, flight),
        out_shape=(
            jax.ShapeDtypeStruct((rows, ids.shape[1]), jnp.bfloat16),
            jax.ShapeDtypeStruct((rows, LANES), jnp.float32),
            jax.ShapeDtypeStruct((rows, LANES), jnp.float32),
        ),
        in_specs=[VMEM],
        out_specs=(VMEM,) * 3,
        compiler_params=pltpu.CompilerParams(vmem_limit_bytes=2 << 20),
        cost_estimate=pl.CostEstimate(flops=10**9, bytes_accessed=0, transcendentals=0),
        name="route",
    )(routes)
    taken = pl.pallas_call(
        select_kernel,
        out_shape=jax.ShapeDtypeStruct((rows, width), jnp.bfloat16),
        in_specs=[VMEM] * 4,
        out_specs=VMEM,
        compiler_params=pltpu.CompilerParams(vmem_limit_bytes=2 << 20),
        name="select",
    )(chooser, scale, inputs, cotan)
    return taken, slots


def join_kernel(*refs):
    out_ref, start = refs[-1], 0
    for ref in refs[:-1]:
        out_ref[pl.ds(start, ref.shape[0]), :] = ref[...]
        start += ref.shape[0]


def join(*pieces):
    rows, width = sum(piece.shape[0] for piece in pieces), pieces[0].shape[1]
    return pl.pallas_call(
        join_kernel,
        out_shape=jax.ShapeDtypeStruct((rows, width), pieces[0].dtype),
        in_specs=[VMEM] * len(pieces),
        out_specs=VMEM,
        compiler_params=pltpu.CompilerParams(vmem_limit_bytes=1 << 20),
        cost_estimate=pl.CostEstimate(flops=10**10, bytes_accessed=0, transcendentals=0),
        name="join",
    )(*pieces)


def main_kernel(pieces, split, *refs):
    row_refs, refs = refs[:pieces], refs[pieces:]
    slots_ref, gate_ref, up_ref, down_ref = refs[:4]
    all_ref, gate_out, up_out, hidden_out = refs[4:8]
    partial_refs = refs[8:]
    start = 0
    for ref in row_refs:
        all_ref[pl.ds(start, ref.shape[0]), :] = ref[...]
        start += ref.shape[0]
    rows = all_ref[...]
    total = rows.shape[0]

    def packed(value):
        moved = pltpu.roll(value, CAP, 0)
        return jnp.concatenate(
            [
                value[2 * m * PAIR : (2 * m + 1) * PAIR]
                + moved[(2 * m + 1) * PAIR : (2 * m + 2) * PAIR]
                for m in range(total // PAIR // 2)
            ],
            axis=0,
        ).astype(jnp.bfloat16)

    units, width = gate_ref.shape
    lefts = []
    for start in range(0, units, UNIT_CHUNK):
        part = slice(start, min(start + UNIT_CHUNK, units))
        pre_gate = contract_last(rows, gate_ref[part])
        pre_up = contract_last(rows, up_ref[part])
        hidden_grad = pltpu.roll(contract_last(rows, down_ref[part]), total - CAP, 0)
        sigma = jax.nn.sigmoid(pre_gate)
        silu_val = pre_gate * sigma
        silu_grad = sigma * (1.0 + pre_gate * (1.0 - sigma))
        first = lax.rem(lax.broadcasted_iota(jnp.int32, pre_gate.shape, 0), PAIR) < CAP
        hidden = jnp.where(first, silu_val * pre_up, 0.0)
        grad_gate = jnp.where(first, hidden_grad * pre_up * silu_grad, 0.0)
        grad_up = jnp.where(first, hidden_grad * silu_val, 0.0)
        gate_out[:, part] = grad_gate.astype(jnp.bfloat16)
        up_out[:, part] = grad_up.astype(jnp.bfloat16)
        hidden_out[:, part] = pltpu.roll(hidden, CAP, 0).astype(jnp.bfloat16)
        lefts.append((part, packed(grad_gate), packed(grad_up)))
    for start in range(0, width, WIDTH_CHUNK):
        columns = slice(start, min(start + WIDTH_CHUNK, width))
        partial = jnp.zeros((total // 2, columns.stop - start), jnp.float32)
        for part, gate_rows, up_rows in lefts:
            for left, weight_ref in ((gate_rows, gate_ref), (up_rows, up_ref)):
                partial = partial + jnp.dot(
                    left, weight_ref[part, columns], preferred_element_type=jnp.float32
                )
        partial = partial.astype(jnp.bfloat16)
        if split:
            half = total // 4
            partial_refs[0][:, columns] = partial[:half]
            partial_refs[1][:, columns] = partial[half:]
        else:
            partial_refs[0][:, columns] = partial
    if split:
        keep_ref = partial_refs[0]
        keep_ref[:PAIR, width:] = slots_ref[...].astype(jnp.bfloat16)
        keep_ref[PAIR:, width:] = jnp.zeros((half - PAIR, LANES), jnp.bfloat16)


def expert_main(pieces, slots, weight_gate, weight_up, weight_down, split):
    total = sum(piece.shape[0] for piece in pieces)
    units, width = weight_gate.shape
    rows = total // 2
    small = jax.ShapeDtypeStruct((total, units), jnp.bfloat16)
    if split:
        partials = (
            jax.ShapeDtypeStruct((rows // 2, width + LANES), jnp.bfloat16),
            jax.ShapeDtypeStruct((rows // 2, width), jnp.bfloat16),
        )
    else:
        partials = (jax.ShapeDtypeStruct((rows, width), jnp.bfloat16),)
    outs = (jax.ShapeDtypeStruct((total, width), jnp.bfloat16), small, small, small) + partials
    return pl.pallas_call(
        functools.partial(main_kernel, len(pieces), split),
        out_shape=outs,
        in_specs=[VMEM] * (len(pieces) + 4),
        out_specs=(VMEM,) * len(outs),
        compiler_params=pltpu.CompilerParams(vmem_limit_bytes=32 << 20),
        cost_estimate=pl.CostEstimate(
            flops=2 * total * units * width * 5,
            bytes_accessed=3 * units * width * 2,
            transcendentals=total * units,
        ),
        name="expert_main",
    )(*pieces, slots, weight_gate, weight_up, weight_down)


def grad_kernel(count, *refs):
    lefts, rows_ref, outs = refs[:count], refs[count], refs[count + 1 : 2 * count + 1]
    held_ref, sems = refs[2 * count + 1 :]
    width = rows_ref.shape[1]
    copies = []
    for j in range(count):
        left = lefts[j][...]
        for c, start in enumerate(range(0, width, CHUNK)):
            part = pl.ds(start, min(CHUNK, width - start))
            held_ref[j, :, part] = contract_first(left, rows_ref[:, part]).astype(jnp.bfloat16)
            copy = pltpu.make_async_copy(
                held_ref.at[j, :, part], outs[j].at[:, part], sems.at[j, c]
            )
            copy.start()
            copies.append(copy)
    for copy in copies:
        copy.wait()


def weight_grads(rows, *lefts):
    total, width = rows.shape
    units = lefts[0].shape[1]
    count = len(lefts)
    return pl.pallas_call(
        functools.partial(grad_kernel, count),
        out_shape=(jax.ShapeDtypeStruct((units, width), jnp.bfloat16),) * count,
        in_specs=[VMEM] * (count + 1),
        out_specs=(HBM,) * count,
        scratch_shapes=[
            pltpu.VMEM((count, units, width), jnp.bfloat16),
            pltpu.SemaphoreType.DMA((count, pl.cdiv(width, CHUNK))),
        ],
        compiler_params=pltpu.CompilerParams(vmem_limit_bytes=24 << 20),
        cost_estimate=pl.CostEstimate(
            flops=2 * total * units * width * count,
            bytes_accessed=units * width * 4 * count,
            transcendentals=0,
        ),
        name="weight_grads",
    )(*lefts, rows)


def expand_kernel(kept_ref, *refs):
    homes, out_ref = refs[:-1], refs[-1]
    tokens, width = out_ref.shape
    combined = kept_ref[:, :width]
    for home in homes:
        combined = combined + home[...].astype(jnp.float32)
    numbers = kept_ref[:, width : width + 1]
    column = lax.broadcasted_iota(jnp.int32, (CAP, tokens), 1).astype(jnp.float32)
    chooser = jnp.where(column == numbers, 1.0, 0.0).astype(jnp.bfloat16)
    out_ref[...] = contract_first(chooser, combined.astype(jnp.bfloat16)).astype(jnp.bfloat16)


def expand(kept, homes, tokens, width):
    return pl.pallas_call(
        expand_kernel,
        out_shape=jax.ShapeDtypeStruct((tokens, width), jnp.bfloat16),
        in_specs=[VMEM] * (len(homes) + 1),
        out_specs=VMEM,
        compiler_params=pltpu.CompilerParams(vmem_limit_bytes=8 << 20),
        name="expand",
    )(kept, *homes)


def swap(value, bits):
    peers = lax.axis_size("expert")
    return lax.ppermute(value, "expert", [(i, i ^ bits) for i in range(peers)])


def shift_back(value, bits):
    count, peers = lax.axis_size("pipe"), lax.axis_size("expert")
    pairs = [
        (section * peers + i, (section - 1) * peers + (i ^ bits))
        for section in range(1, count)
        for i in range(peers)
    ]
    return lax.ppermute(value, ("pipe", "expert"), pairs)


def one_expert(own, slots, weights, tokens, width):
    first, second, third = (swap(own, bits) for bits in OUT)
    across = [swap(join(own, first, second), 1)]
    across.append(swap(third, 1))
    pieces = (own, first, second, third, *across)
    rows, gate, up, hidden, keep, send = expert_main(pieces, slots, *weights, split=True)
    beside, kept = shift_back(send, 1), shift_back(keep, 0)
    grads = weight_grads(rows, gate, up, hidden)
    kept = kept.astype(jnp.float32)
    summed = kept[:, :width] + beside.astype(jnp.float32)
    rounded = summed.astype(jnp.bfloat16)
    homes = [
        swap(rounded[(OUT.index(bits) + 1) * CAP : (OUT.index(bits) + 2) * CAP], bits)
        for bits in HOME
    ]
    kept = jnp.concatenate([summed[:CAP], kept[:CAP, width:]], axis=1)
    return grads, expand(kept, homes, tokens, width)


def many_experts(own, slots, weights, ids, peers, flight, tokens, width):
    spread = jnp.repeat(own.reshape(flight, PAIR, width), SLICES, axis=0)
    received = lax.all_to_all(spread, "expert", split_axis=0, concat_axis=0, tiled=True)
    received = received.reshape(peers * PAIR, width)
    rows, gate, up, hidden, partial = expert_main((received,), slots, *weights, split=False)
    partial = partial.reshape(peers, CAP, width)
    returned = lax.all_to_all(partial, "expert", split_axis=0, concat_axis=0, tiled=True)
    grads = weight_grads(rows, gate, up, hidden)
    combined = jnp.sum(
        returned.astype(jnp.float32).reshape(flight, SLICES, CAP, width), axis=1
    ).reshape(flight * CAP, width)
    labels = jnp.arange(flight, dtype=jnp.int32)
    named = jnp.any(ids[None] == labels[:, None, None], axis=1)
    ranks = jnp.cumsum(named.astype(jnp.int32), axis=1) - 1
    slot = jnp.arange(CAP, dtype=jnp.int32)
    chooser = named[:, None, :] & (ranks[:, None, :] == slot[None, :, None])
    chooser = chooser.reshape(flight * CAP, tokens).astype(jnp.float32)
    input_grad = lax.dot_general(
        chooser,
        combined,
        (((0,), (0,)), ((), ())),
        precision=lax.Precision.HIGHEST,
        preferred_element_type=jnp.float32,
    )
    return grads, shift_back(input_grad.astype(jnp.bfloat16), 0)


def body(layer_input, grad_output, expert_ids, gate_probs, w_gate, w_up, w_down):
    peers = lax.axis_size("expert")
    flight = peers // SLICES
    tokens, width = layer_input.shape[1:]
    ids = expert_ids[0].T
    weights = (w_gate[0], w_up[0], w_down[0])
    own, slots = select_rows(ids, gate_probs[0].T, layer_input[0], grad_output[0], flight)
    if flight == 1:
        grads, shifted = one_expert(own, slots, weights, tokens, width)
    else:
        grads, shifted = many_experts(
            own, slots, weights, ids, peers, flight, tokens, width
        )
    return tuple(grad[None] for grad in grads) + (shifted[None],)


def solution(mesh):
    spec = P("pipe", "expert", None)
    return jax.shard_map(
        body, mesh=mesh, in_specs=(spec,) * 7, out_specs=(spec,) * 4, check_vma=False
    )
```

```python
import functools

import jax
import jax.numpy as jnp
from jax import lax
from jax.experimental import pallas as pl
from jax.experimental.pallas import tpu as pltpu
from jax.sharding import PartitionSpec as P


SLICES = 8
CAP = 4
PAIR = 2 * CAP
LANES = 128
CHUNK = 1024
UNIT_CHUNK = 256
WIDTH_CHUNK = 1536
OUT = (4, 2, 6)
HOME = (4, 6, 2)

VMEM = pl.BlockSpec(memory_space=pltpu.VMEM)
HBM = pl.BlockSpec(memory_space=pl.ANY)


def contract_last(left, right):
    return lax.dot_general(
        left, right, (((1,), (1,)), ((), ())), preferred_element_type=jnp.float32
    )


def contract_first(left, right):
    return lax.dot_general(
        left, right, (((0,), (0,)), ((), ())), preferred_element_type=jnp.float32
    )


def route_kernel(flight, routes_ref, chooser_ref, scale_ref, slots_ref):
    tokens = routes_ref.shape[2]
    before = lax.broadcasted_iota(jnp.int32, (tokens, tokens), 0) < lax.broadcasted_iota(
        jnp.int32, (tokens, tokens), 1
    )
    before = before.astype(jnp.float32).astype(jnp.bfloat16)
    row = lax.broadcasted_iota(jnp.int32, (PAIR, tokens), 0)
    token = lax.broadcasted_iota(jnp.int32, (PAIR, tokens), 1).astype(jnp.float32)
    slot = lax.rem(row, CAP)
    for expert in range(flight):
        prob = jnp.sum(routes_ref[expert], axis=0, keepdims=True)
        hits = jnp.broadcast_to(jnp.where(prob > 0.0, 1.0, 0.0), (PAIR, tokens))
        ranks = jnp.dot(hits.astype(jnp.bfloat16), before, preferred_element_type=jnp.float32)
        chosen = jnp.where((hits > 0.5) & (ranks.astype(jnp.int32) == slot), 1.0, 0.0)
        scale = jnp.sum(chosen * prob, axis=1, keepdims=True)
        number = jnp.sum(chosen * token, axis=1, keepdims=True)
        part = pl.ds(expert * PAIR, PAIR)
        slots_ref[part, :] = jnp.broadcast_to(number, (PAIR, LANES))
        scale_ref[part, :] = jnp.broadcast_to(scale, (PAIR, LANES))
        chooser_ref[part, :] = chosen.astype(jnp.bfloat16)


def select_kernel(chooser_ref, scale_ref, input_ref, cotan_ref, rows_ref):
    for start in range(0, rows_ref.shape[0], PAIR):
        part = pl.ds(start, PAIR)
        chooser = chooser_ref[part, :]
        taken = jnp.dot(chooser, input_ref[...], preferred_element_type=jnp.float32)
        cotan = jnp.dot(chooser, cotan_ref[...], preferred_element_type=jnp.float32)
        wide = lax.broadcasted_iota(jnp.int32, taken.shape, 0) < CAP
        rows_ref[part, :] = jnp.where(wide, taken, cotan * scale_ref[part, :1]).astype(
            jnp.bfloat16
        )


def select_rows(ids, probs, inputs, cotan, flight):
    width = inputs.shape[1]
    labels = jnp.arange(flight, dtype=jnp.int32)
    routes = jnp.where(ids[None] == labels[:, None, None], probs[None], 0.0)
    rows = flight * PAIR
    chooser, scale, slots = pl.pallas_call(
        functools.partial(route_kernel, flight),
        out_shape=(
            jax.ShapeDtypeStruct((rows, ids.shape[1]), jnp.bfloat16),
            jax.ShapeDtypeStruct((rows, LANES), jnp.float32),
            jax.ShapeDtypeStruct((rows, LANES), jnp.float32),
        ),
        in_specs=[VMEM],
        out_specs=(VMEM,) * 3,
        compiler_params=pltpu.CompilerParams(vmem_limit_bytes=2 << 20),
        cost_estimate=pl.CostEstimate(flops=10**9, bytes_accessed=0, transcendentals=0),
        name="route",
    )(routes)
    taken = pl.pallas_call(
        select_kernel,
        out_shape=jax.ShapeDtypeStruct((rows, width), jnp.bfloat16),
        in_specs=[VMEM] * 4,
        out_specs=VMEM,
        compiler_params=pltpu.CompilerParams(vmem_limit_bytes=2 << 20),
        name="select",
    )(chooser, scale, inputs, cotan)
    return taken, slots


def join_kernel(*refs):
    out_ref, start = refs[-1], 0
    for ref in refs[:-1]:
        out_ref[pl.ds(start, ref.shape[0]), :] = ref[...]
        start += ref.shape[0]


def join(*pieces):
    rows, width = sum(piece.shape[0] for piece in pieces), pieces[0].shape[1]
    return pl.pallas_call(
        join_kernel,
        out_shape=jax.ShapeDtypeStruct((rows, width), pieces[0].dtype),
        in_specs=[VMEM] * len(pieces),
        out_specs=VMEM,
        compiler_params=pltpu.CompilerParams(vmem_limit_bytes=1 << 20),
        cost_estimate=pl.CostEstimate(flops=10**10, bytes_accessed=0, transcendentals=0),
        name="join",
    )(*pieces)


def main_kernel(pieces, split, *refs):
    row_refs, refs = refs[:pieces], refs[pieces:]
    slots_ref, gate_ref, up_ref, down_ref = refs[:4]
    all_ref, gate_out, up_out, hidden_out = refs[4:8]
    partial_refs = refs[8:]
    start = 0
    for ref in row_refs:
        all_ref[pl.ds(start, ref.shape[0]), :] = ref[...]
        start += ref.shape[0]
    rows = all_ref[...]
    total = rows.shape[0]

    def packed(value):
        moved = pltpu.roll(value, CAP, 0)
        return jnp.concatenate(
            [
                value[2 * m * PAIR : (2 * m + 1) * PAIR]
                + moved[(2 * m + 1) * PAIR : (2 * m + 2) * PAIR]
                for m in range(total // PAIR // 2)
            ],
            axis=0,
        ).astype(jnp.bfloat16)

    units, width = gate_ref.shape
    lefts = []
    for start in range(0, units, UNIT_CHUNK):
        part = slice(start, min(start + UNIT_CHUNK, units))
        pre_gate = contract_last(rows, gate_ref[part])
        pre_up = contract_last(rows, up_ref[part])
        hidden_grad = pltpu.roll(contract_last(rows, down_ref[part]), total - CAP, 0)
        sigma = jax.nn.sigmoid(pre_gate)
        silu_val = pre_gate * sigma
        silu_grad = sigma * (1.0 + pre_gate * (1.0 - sigma))
        first = lax.rem(lax.broadcasted_iota(jnp.int32, pre_gate.shape, 0), PAIR) < CAP
        hidden = jnp.where(first, silu_val * pre_up, 0.0)
        grad_gate = jnp.where(first, hidden_grad * pre_up * silu_grad, 0.0)
        grad_up = jnp.where(first, hidden_grad * silu_val, 0.0)
        gate_out[:, part] = grad_gate.astype(jnp.bfloat16)
        up_out[:, part] = grad_up.astype(jnp.bfloat16)
        hidden_out[:, part] = pltpu.roll(hidden, CAP, 0).astype(jnp.bfloat16)
        lefts.append((part, packed(grad_gate), packed(grad_up)))
    for start in range(0, width, WIDTH_CHUNK):
        columns = slice(start, min(start + WIDTH_CHUNK, width))
        partial = jnp.zeros((total // 2, columns.stop - start), jnp.float32)
        for part, gate_rows, up_rows in lefts:
            for left, weight_ref in ((gate_rows, gate_ref), (up_rows, up_ref)):
                partial = partial + jnp.dot(
                    left, weight_ref[part, columns], preferred_element_type=jnp.float32
                )
        partial = partial.astype(jnp.bfloat16)
        if split:
            half = total // 4
            partial_refs[0][:, columns] = partial[:half]
            partial_refs[1][:, columns] = partial[half:]
        else:
            partial_refs[0][:, columns] = partial
    if split:
        keep_ref = partial_refs[0]
        keep_ref[:PAIR, width:] = slots_ref[...].astype(jnp.bfloat16)
        keep_ref[PAIR:, width:] = jnp.zeros((half - PAIR, LANES), jnp.bfloat16)


def expert_main(pieces, slots, weight_gate, weight_up, weight_down, split):
    total = sum(piece.shape[0] for piece in pieces)
    units, width = weight_gate.shape
    rows = total // 2
    small = jax.ShapeDtypeStruct((total, units), jnp.bfloat16)
    if split:
        partials = (
            jax.ShapeDtypeStruct((rows // 2, width + LANES), jnp.bfloat16),
            jax.ShapeDtypeStruct((rows // 2, width), jnp.bfloat16),
        )
    else:
        partials = (jax.ShapeDtypeStruct((rows, width), jnp.bfloat16),)
    outs = (jax.ShapeDtypeStruct((total, width), jnp.bfloat16), small, small, small) + partials
    return pl.pallas_call(
        functools.partial(main_kernel, len(pieces), split),
        out_shape=outs,
        in_specs=[VMEM] * (len(pieces) + 4),
        out_specs=(VMEM,) * len(outs),
        compiler_params=pltpu.CompilerParams(vmem_limit_bytes=32 << 20),
        cost_estimate=pl.CostEstimate(
            flops=2 * total * units * width * 5,
            bytes_accessed=3 * units * width * 2,
            transcendentals=total * units,
        ),
        name="expert_main",
    )(*pieces, slots, weight_gate, weight_up, weight_down)


def grad_kernel(count, *refs):
    lefts, rows_ref, outs = refs[:count], refs[count], refs[count + 1 : 2 * count + 1]
    held_ref, sems = refs[2 * count + 1 :]
    width = rows_ref.shape[1]
    copies = []
    for j in range(count):
        left = lefts[j][...]
        for c, start in enumerate(range(0, width, CHUNK)):
            part = pl.ds(start, min(CHUNK, width - start))
            held_ref[j, :, part] = contract_first(left, rows_ref[:, part]).astype(jnp.bfloat16)
            copy = pltpu.make_async_copy(
                held_ref.at[j, :, part], outs[j].at[:, part], sems.at[j, c]
            )
            copy.start()
            copies.append(copy)
    for copy in copies:
        copy.wait()


def weight_grads(rows, *lefts):
    total, width = rows.shape
    units = lefts[0].shape[1]
    count = len(lefts)
    return pl.pallas_call(
        functools.partial(grad_kernel, count),
        out_shape=(jax.ShapeDtypeStruct((units, width), jnp.bfloat16),) * count,
        in_specs=[VMEM] * (count + 1),
        out_specs=(HBM,) * count,
        scratch_shapes=[
            pltpu.VMEM((count, units, width), jnp.bfloat16),
            pltpu.SemaphoreType.DMA((count, pl.cdiv(width, CHUNK))),
        ],
        compiler_params=pltpu.CompilerParams(vmem_limit_bytes=24 << 20),
        cost_estimate=pl.CostEstimate(
            flops=2 * total * units * width * count,
            bytes_accessed=units * width * 4 * count,
            transcendentals=0,
        ),
        name="weight_grads",
    )(*lefts, rows)


def expand_kernel(kept_ref, *refs):
    homes, out_ref = refs[:-1], refs[-1]
    tokens, width = out_ref.shape
    combined = kept_ref[:, :width]
    for home in homes:
        combined = combined + home[...].astype(jnp.float32)
    numbers = kept_ref[:, width : width + 1]
    column = lax.broadcasted_iota(jnp.int32, (CAP, tokens), 1).astype(jnp.float32)
    chooser = jnp.where(column == numbers, 1.0, 0.0).astype(jnp.bfloat16)
    out_ref[...] = contract_first(chooser, combined.astype(jnp.bfloat16)).astype(jnp.bfloat16)


def expand(kept, homes, tokens, width):
    return pl.pallas_call(
        expand_kernel,
        out_shape=jax.ShapeDtypeStruct((tokens, width), jnp.bfloat16),
        in_specs=[VMEM] * (len(homes) + 1),
        out_specs=VMEM,
        compiler_params=pltpu.CompilerParams(vmem_limit_bytes=8 << 20),
        name="expand",
    )(kept, *homes)


def swap(value, bits):
    peers = lax.axis_size("expert")
    return lax.ppermute(value, "expert", [(i, i ^ bits) for i in range(peers)])


def shift_back(value, bits):
    count, peers = lax.axis_size("pipe"), lax.axis_size("expert")
    pairs = [
        (section * peers + i, (section - 1) * peers + (i ^ bits))
        for section in range(1, count)
        for i in range(peers)
    ]
    return lax.ppermute(value, ("pipe", "expert"), pairs)


def one_expert(own, slots, weights, tokens, width):
    far = swap(own, 4)
    across, along = swap(own, 1), swap(own, 2)
    over = swap(join(own, far), 3)
    along_far, across_far = swap(far, 2), swap(far, 1)
    pieces = (own, far, along, along_far, across, across_far, over)
    rows, gate, up, hidden, keep, send = expert_main(pieces, slots, *weights, split=True)
    beside, kept = shift_back(send, 1), shift_back(keep, 0)
    grads = weight_grads(rows, gate, up, hidden)
    kept = kept.astype(jnp.float32)
    summed = kept[:, :width] + beside.astype(jnp.float32)
    rounded = summed.astype(jnp.bfloat16)
    homes = [
        swap(rounded[(OUT.index(bits) + 1) * CAP : (OUT.index(bits) + 2) * CAP], bits)
        for bits in HOME
    ]
    kept = jnp.concatenate([summed[:CAP], kept[:CAP, width:]], axis=1)
    return grads, expand(kept, homes, tokens, width)


def many_experts(own, slots, weights, ids, peers, flight, tokens, width):
    spread = jnp.repeat(own.reshape(flight, PAIR, width), SLICES, axis=0)
    received = lax.all_to_all(spread, "expert", split_axis=0, concat_axis=0, tiled=True)
    received = received.reshape(peers * PAIR, width)
    rows, gate, up, hidden, partial = expert_main((received,), slots, *weights, split=False)
    partial = partial.reshape(peers, CAP, width)
    returned = lax.all_to_all(partial, "expert", split_axis=0, concat_axis=0, tiled=True)
    grads = weight_grads(rows, gate, up, hidden)
    combined = jnp.sum(
        returned.astype(jnp.float32).reshape(flight, SLICES, CAP, width), axis=1
    ).reshape(flight * CAP, width)
    labels = jnp.arange(flight, dtype=jnp.int32)
    named = jnp.any(ids[None] == labels[:, None, None], axis=1)
    ranks = jnp.cumsum(named.astype(jnp.int32), axis=1) - 1
    slot = jnp.arange(CAP, dtype=jnp.int32)
    chooser = named[:, None, :] & (ranks[:, None, :] == slot[None, :, None])
    chooser = chooser.reshape(flight * CAP, tokens).astype(jnp.float32)
    input_grad = lax.dot_general(
        chooser,
        combined,
        (((0,), (0,)), ((), ())),
        precision=lax.Precision.HIGHEST,
        preferred_element_type=jnp.float32,
    )
    return grads, shift_back(input_grad.astype(jnp.bfloat16), 0)


def body(layer_input, grad_output, expert_ids, gate_probs, w_gate, w_up, w_down):
    peers = lax.axis_size("expert")
    flight = peers // SLICES
    tokens, width = layer_input.shape[1:]
    ids = expert_ids[0].T
    weights = (w_gate[0], w_up[0], w_down[0])
    own, slots = select_rows(ids, gate_probs[0].T, layer_input[0], grad_output[0], flight)
    if flight == 1:
        grads, shifted = one_expert(own, slots, weights, tokens, width)
    else:
        grads, shifted = many_experts(
            own, slots, weights, ids, peers, flight, tokens, width
        )
    return tuple(grad[None] for grad in grads) + (shifted[None],)


def solution(mesh):
    spec = P("pipe", "expert", None)
    return jax.shard_map(
        body, mesh=mesh, in_specs=(spec,) * 7, out_specs=(spec,) * 4, check_vma=False
    )
```

```python
import functools

import jax
import jax.numpy as jnp
from jax import lax
from jax.experimental import pallas as pl
from jax.experimental.pallas import tpu as pltpu
from jax.sharding import PartitionSpec as P


SLICES = 8
CAP = 4
PAIR = 2 * CAP
LANES = 128
CHUNK = 512
EXPAND_CHUNK = 1024
UNIT_CHUNK = 256
WIDTH_CHUNK = 1536
OUT = (4, 2, 6)
HOME = (4, 6, 2)

VMEM = pl.BlockSpec(memory_space=pltpu.VMEM)
HBM = pl.BlockSpec(memory_space=pl.ANY)


def contract_last(left, right):
    return lax.dot_general(
        left, right, (((1,), (1,)), ((), ())), preferred_element_type=jnp.float32
    )


def contract_first(left, right):
    return lax.dot_general(
        left, right, (((0,), (0,)), ((), ())), preferred_element_type=jnp.float32
    )


def route_kernel(flight, routes_ref, chooser_ref, scale_ref, slots_ref):
    tokens = routes_ref.shape[2]
    before = lax.broadcasted_iota(jnp.int32, (tokens, tokens), 0) < lax.broadcasted_iota(
        jnp.int32, (tokens, tokens), 1
    )
    before = before.astype(jnp.float32).astype(jnp.bfloat16)
    row = lax.broadcasted_iota(jnp.int32, (PAIR, tokens), 0)
    token = lax.broadcasted_iota(jnp.int32, (PAIR, tokens), 1).astype(jnp.float32)
    slot = lax.rem(row, CAP)
    for expert in range(flight):
        prob = jnp.sum(routes_ref[expert], axis=0, keepdims=True)
        hits = jnp.broadcast_to(jnp.where(prob > 0.0, 1.0, 0.0), (PAIR, tokens))
        ranks = jnp.dot(hits.astype(jnp.bfloat16), before, preferred_element_type=jnp.float32)
        chosen = jnp.where((hits > 0.5) & (ranks.astype(jnp.int32) == slot), 1.0, 0.0)
        scale = jnp.sum(chosen * prob, axis=1, keepdims=True)
        number = jnp.sum(chosen * token, axis=1, keepdims=True)
        part = pl.ds(expert * PAIR, PAIR)
        slots_ref[part, :] = jnp.broadcast_to(number, (PAIR, LANES))
        scale_ref[part, :] = jnp.broadcast_to(scale, (PAIR, LANES))
        chooser_ref[part, :] = chosen.astype(jnp.bfloat16)


def select_kernel(chooser_ref, scale_ref, input_ref, cotan_ref, rows_ref):
    for start in range(0, rows_ref.shape[0], PAIR):
        part = pl.ds(start, PAIR)
        chooser = chooser_ref[part, :]
        taken = jnp.dot(chooser, input_ref[...], preferred_element_type=jnp.float32)
        cotan = jnp.dot(chooser, cotan_ref[...], preferred_element_type=jnp.float32)
        wide = lax.broadcasted_iota(jnp.int32, taken.shape, 0) < CAP
        rows_ref[part, :] = jnp.where(wide, taken, cotan * scale_ref[part, :1]).astype(
            jnp.bfloat16
        )


def select_rows(ids, probs, inputs, cotan, flight):
    width = inputs.shape[1]
    labels = jnp.arange(flight, dtype=jnp.int32)
    routes = jnp.where(ids[None] == labels[:, None, None], probs[None], 0.0)
    rows = flight * PAIR
    chooser, scale, slots = pl.pallas_call(
        functools.partial(route_kernel, flight),
        out_shape=(
            jax.ShapeDtypeStruct((rows, ids.shape[1]), jnp.bfloat16),
            jax.ShapeDtypeStruct((rows, LANES), jnp.float32),
            jax.ShapeDtypeStruct((rows, LANES), jnp.float32),
        ),
        in_specs=[VMEM],
        out_specs=(VMEM,) * 3,
        compiler_params=pltpu.CompilerParams(vmem_limit_bytes=2 << 20),
        cost_estimate=pl.CostEstimate(flops=10**9, bytes_accessed=0, transcendentals=0),
        name="route",
    )(routes)
    taken = pl.pallas_call(
        select_kernel,
        out_shape=jax.ShapeDtypeStruct((rows, width), jnp.bfloat16),
        in_specs=[VMEM] * 4,
        out_specs=VMEM,
        compiler_params=pltpu.CompilerParams(vmem_limit_bytes=2 << 20),
        name="select",
    )(chooser, scale, inputs, cotan)
    return taken, slots


def join_kernel(*refs):
    out_ref, start = refs[-1], 0
    for ref in refs[:-1]:
        out_ref[pl.ds(start, ref.shape[0]), :] = ref[...]
        start += ref.shape[0]


def join(*pieces):
    rows, width = sum(piece.shape[0] for piece in pieces), pieces[0].shape[1]
    return pl.pallas_call(
        join_kernel,
        out_shape=jax.ShapeDtypeStruct((rows, width), pieces[0].dtype),
        in_specs=[VMEM] * len(pieces),
        out_specs=VMEM,
        compiler_params=pltpu.CompilerParams(vmem_limit_bytes=1 << 20),
        cost_estimate=pl.CostEstimate(flops=10**10, bytes_accessed=0, transcendentals=0),
        name="join",
    )(*pieces)


def main_kernel(pieces, split, *refs):
    row_refs, refs = refs[:pieces], refs[pieces:]
    slots_ref, gate_ref, up_ref, down_ref = refs[:4]
    all_ref, gate_out, up_out, hidden_out = refs[4:8]
    partial_refs = refs[8:]
    start = 0
    for ref in row_refs:
        all_ref[pl.ds(start, ref.shape[0]), :] = ref[...]
        start += ref.shape[0]
    rows = all_ref[...]
    total = rows.shape[0]

    def packed(value):
        moved = pltpu.roll(value, CAP, 0)
        return jnp.concatenate(
            [
                value[2 * m * PAIR : (2 * m + 1) * PAIR]
                + moved[(2 * m + 1) * PAIR : (2 * m + 2) * PAIR]
                for m in range(total // PAIR // 2)
            ],
            axis=0,
        ).astype(jnp.bfloat16)

    units, width = gate_ref.shape
    lefts = []
    for start in range(0, units, UNIT_CHUNK):
        part = slice(start, min(start + UNIT_CHUNK, units))
        pre_gate = contract_last(rows, gate_ref[part])
        pre_up = contract_last(rows, up_ref[part])
        hidden_grad = pltpu.roll(contract_last(rows, down_ref[part]), total - CAP, 0)
        sigma = jax.nn.sigmoid(pre_gate)
        silu_val = pre_gate * sigma
        silu_grad = sigma * (1.0 + pre_gate * (1.0 - sigma))
        first = lax.rem(lax.broadcasted_iota(jnp.int32, pre_gate.shape, 0), PAIR) < CAP
        hidden = jnp.where(first, silu_val * pre_up, 0.0)
        grad_gate = jnp.where(first, hidden_grad * pre_up * silu_grad, 0.0)
        grad_up = jnp.where(first, hidden_grad * silu_val, 0.0)
        gate_out[:, part] = grad_gate.astype(jnp.bfloat16)
        up_out[:, part] = grad_up.astype(jnp.bfloat16)
        hidden_out[:, part] = pltpu.roll(hidden, CAP, 0).astype(jnp.bfloat16)
        lefts.append((part, packed(grad_gate), packed(grad_up)))
    for start in range(0, width, WIDTH_CHUNK):
        columns = slice(start, min(start + WIDTH_CHUNK, width))
        partial = jnp.zeros((total // 2, columns.stop - start), jnp.float32)
        for part, gate_rows, up_rows in lefts:
            for left, weight_ref in ((gate_rows, gate_ref), (up_rows, up_ref)):
                partial = partial + jnp.dot(
                    left, weight_ref[part, columns], preferred_element_type=jnp.float32
                )
        partial = partial.astype(jnp.bfloat16)
        if split:
            half = total // 4
            partial_refs[0][:, columns] = partial[:half]
            partial_refs[1][:, columns] = partial[half:]
        else:
            partial_refs[0][:, columns] = partial
    if split:
        keep_ref = partial_refs[0]
        keep_ref[:PAIR, width:] = slots_ref[...].astype(jnp.bfloat16)
        keep_ref[PAIR:, width:] = jnp.zeros((half - PAIR, LANES), jnp.bfloat16)


def expert_main(pieces, slots, weight_gate, weight_up, weight_down, split):
    total = sum(piece.shape[0] for piece in pieces)
    units, width = weight_gate.shape
    rows = total // 2
    small = jax.ShapeDtypeStruct((total, units), jnp.bfloat16)
    if split:
        partials = (
            jax.ShapeDtypeStruct((rows // 2, width + LANES), jnp.bfloat16),
            jax.ShapeDtypeStruct((rows // 2, width), jnp.bfloat16),
        )
    else:
        partials = (jax.ShapeDtypeStruct((rows, width), jnp.bfloat16),)
    outs = (jax.ShapeDtypeStruct((total, width), jnp.bfloat16), small, small, small) + partials
    return pl.pallas_call(
        functools.partial(main_kernel, len(pieces), split),
        out_shape=outs,
        in_specs=[VMEM] * (len(pieces) + 4),
        out_specs=(VMEM,) * len(outs),
        compiler_params=pltpu.CompilerParams(vmem_limit_bytes=32 << 20),
        cost_estimate=pl.CostEstimate(
            flops=2 * total * units * width * 5,
            bytes_accessed=3 * units * width * 2,
            transcendentals=total * units,
        ),
        name="expert_main",
    )(*pieces, slots, weight_gate, weight_up, weight_down)


def grad_kernel(count, *refs):
    lefts, rows_ref, outs = refs[:count], refs[count], refs[count + 1 : 2 * count + 1]
    held_ref, sems = refs[2 * count + 1 :]
    width = rows_ref.shape[1]
    copies = []
    for j in range(count):
        left = lefts[j][...]
        for c, start in enumerate(range(0, width, CHUNK)):
            part = pl.ds(start, min(CHUNK, width - start))
            held_ref[j, :, part] = contract_first(left, rows_ref[:, part]).astype(jnp.bfloat16)
            copy = pltpu.make_async_copy(
                held_ref.at[j, :, part], outs[j].at[:, part], sems.at[j, c]
            )
            copy.start()
            copies.append(copy)
    for copy in copies:
        copy.wait()


def weight_grads(rows, *lefts):
    total, width = rows.shape
    units = lefts[0].shape[1]
    count = len(lefts)
    return pl.pallas_call(
        functools.partial(grad_kernel, count),
        out_shape=(jax.ShapeDtypeStruct((units, width), jnp.bfloat16),) * count,
        in_specs=[VMEM] * (count + 1),
        out_specs=(HBM,) * count,
        scratch_shapes=[
            pltpu.VMEM((count, units, width), jnp.bfloat16),
            pltpu.SemaphoreType.DMA((count, pl.cdiv(width, CHUNK))),
        ],
        compiler_params=pltpu.CompilerParams(vmem_limit_bytes=24 << 20),
        cost_estimate=pl.CostEstimate(
            flops=2 * total * units * width * count,
            bytes_accessed=units * width * 4 * count,
            transcendentals=0,
        ),
        name="weight_grads",
    )(*lefts, rows)


def expand_kernel(kept_ref, *refs):
    homes, (out_ref, held_ref, sems) = refs[:-3], refs[-3:]
    tokens, width = out_ref.shape
    numbers = kept_ref[:, width : width + 1]
    column = lax.broadcasted_iota(jnp.int32, (CAP, tokens), 1).astype(jnp.float32)
    chooser = jnp.where(column == numbers, 1.0, 0.0).astype(jnp.bfloat16)
    copies = []
    for c, start in enumerate(range(0, width, EXPAND_CHUNK)):
        part = pl.ds(start, min(EXPAND_CHUNK, width - start))
        combined = kept_ref[:, part]
        for home in homes:
            combined = combined + home[:, part].astype(jnp.float32)
        held_ref[:, part] = contract_first(chooser, combined.astype(jnp.bfloat16)).astype(
            jnp.bfloat16
        )
        copies.append(
            pltpu.make_async_copy(held_ref.at[:, part], out_ref.at[:, part], sems.at[c])
        )
        copies[-1].start()
    for copy in copies:
        copy.wait()


def expand(kept, homes, tokens, width):
    return pl.pallas_call(
        expand_kernel,
        out_shape=jax.ShapeDtypeStruct((tokens, width), jnp.bfloat16),
        in_specs=[VMEM] * (len(homes) + 1),
        out_specs=HBM,
        scratch_shapes=[
            pltpu.VMEM((tokens, width), jnp.bfloat16),
            pltpu.SemaphoreType.DMA((pl.cdiv(width, EXPAND_CHUNK),)),
        ],
        compiler_params=pltpu.CompilerParams(vmem_limit_bytes=8 << 20),
        name="expand",
    )(kept, *homes)


def swap(value, bits):
    peers = lax.axis_size("expert")
    return lax.ppermute(value, "expert", [(i, i ^ bits) for i in range(peers)])


def shift_back(value, bits):
    count, peers = lax.axis_size("pipe"), lax.axis_size("expert")
    pairs = [
        (section * peers + i, (section - 1) * peers + (i ^ bits))
        for section in range(1, count)
        for i in range(peers)
    ]
    return lax.ppermute(value, ("pipe", "expert"), pairs)


def one_expert(own, slots, weights, tokens, width):
    far = swap(own, 4)
    across, along = swap(own, 1), swap(own, 2)
    over = swap(join(own, far), 3)
    along_far, across_far = swap(far, 2), swap(far, 1)
    pieces = (own, far, along, along_far, across, across_far, over)
    rows, gate, up, hidden, keep, send = expert_main(pieces, slots, *weights, split=True)
    beside, kept = shift_back(send, 1), shift_back(keep, 0)
    grads = weight_grads(rows, gate, up)
    grads += weight_grads(rows, hidden)
    kept = kept.astype(jnp.float32)
    summed = kept[:, :width] + beside.astype(jnp.float32)
    rounded = summed.astype(jnp.bfloat16)
    homes = [
        swap(rounded[(OUT.index(bits) + 1) * CAP : (OUT.index(bits) + 2) * CAP], bits)
        for bits in HOME
    ]
    kept = jnp.concatenate([summed[:CAP], kept[:CAP, width:]], axis=1)
    return grads, expand(kept, homes, tokens, width)


def many_experts(own, slots, weights, ids, peers, flight, tokens, width):
    spread = jnp.repeat(own.reshape(flight, PAIR, width), SLICES, axis=0)
    received = lax.all_to_all(spread, "expert", split_axis=0, concat_axis=0, tiled=True)
    received = received.reshape(peers * PAIR, width)
    rows, gate, up, hidden, partial = expert_main((received,), slots, *weights, split=False)
    partial = partial.reshape(peers, CAP, width)
    returned = lax.all_to_all(partial, "expert", split_axis=0, concat_axis=0, tiled=True)
    grads = weight_grads(rows, gate, up, hidden)
    combined = jnp.sum(
        returned.astype(jnp.float32).reshape(flight, SLICES, CAP, width), axis=1
    ).reshape(flight * CAP, width)
    labels = jnp.arange(flight, dtype=jnp.int32)
    named = jnp.any(ids[None] == labels[:, None, None], axis=1)
    ranks = jnp.cumsum(named.astype(jnp.int32), axis=1) - 1
    slot = jnp.arange(CAP, dtype=jnp.int32)
    chooser = named[:, None, :] & (ranks[:, None, :] == slot[None, :, None])
    chooser = chooser.reshape(flight * CAP, tokens).astype(jnp.float32)
    input_grad = lax.dot_general(
        chooser,
        combined,
        (((0,), (0,)), ((), ())),
        precision=lax.Precision.HIGHEST,
        preferred_element_type=jnp.float32,
    )
    return grads, shift_back(input_grad.astype(jnp.bfloat16), 0)


def body(layer_input, grad_output, expert_ids, gate_probs, w_gate, w_up, w_down):
    peers = lax.axis_size("expert")
    flight = peers // SLICES
    tokens, width = layer_input.shape[1:]
    ids = expert_ids[0].T
    weights = (w_gate[0], w_up[0], w_down[0])
    own, slots = select_rows(ids, gate_probs[0].T, layer_input[0], grad_output[0], flight)
    if flight == 1:
        grads, shifted = one_expert(own, slots, weights, tokens, width)
    else:
        grads, shifted = many_experts(
            own, slots, weights, ids, peers, flight, tokens, width
        )
    return tuple(grad[None] for grad in grads) + (shifted[None],)


def solution(mesh):
    spec = P("pipe", "expert", None)
    return jax.shard_map(
        body, mesh=mesh, in_specs=(spec,) * 7, out_specs=(spec,) * 4, check_vma=False
    )
```
